32 devices in a mesh: groups: 2 (over x), facet: 16 (over z, y, core).
Axes of the slice: x: 2, y: 2, z: 4, core: 2. Of those that a mesh axis runs over, the one named last changes fastest.
Arguments:
- facets: bfloat16 [32, 2, 512, 512], P(('groups', 'facet')), parts along dimension 0, may hold values from -6 to 6
- facet_offsets: int32 [32, 2], P(('groups', 'facet')), parts along dimension 0, may hold values from 0 to 511
- subgrid_offsets: int32 [32, 2], P('groups'), parts along dimension 0, may hold values from 0 to 511
- w_terms: float32 [32], P(('groups', 'facet')), parts along dimension 0, may hold values from 2 to 16
- tile_count: int32 [32], P(('groups', 'facet')), parts along dimension 0, may hold values from 1 to 16, as said below
- tile_offsets: int32 [512, 2], P(('groups', 'facet')), parts along dimension 0, may hold values from 0 to 256
- observed: bfloat16 [512, 2, 128, 128], P(('groups', 'facet')), parts along dimension 0, may hold values from -6 to 6
Outputs:
- residual: bfloat16 [512, 2, 128, 128], P(('groups', 'facet')), parts along dimension 0
- facet_update: bfloat16 [32, 2, 512, 512], P(('groups', 'facet')), parts along dimension 0
The draws below stay inside these ranges and needn't reach their ends.
There are 2 independent parts, one for each index of `groups`. The reference program is written for one: setup_inputs(seed, part) draws one part's arguments, and reference() takes and returns one part's arrays. A program takes and returns all parts, laid end to end along the dimension named above; each array names one. Nothing has to cross between parts.
Inputs may be any that keep to these rules, and one draw needn't show every extreme that they name: `tile_count`: live tile slots of each subgrid; some subgrid has all 16 slots live in every draw.
All inputs are finite; a program needn't handle non-finite values.
Results may differ from the reference program's by a relative error of at most 0.017.
Values may be sent and summed in bfloat16 or wider, within the bound.
A program may use at most 64 MiB of HBM per device.

```python
import math
import jax
import jax.numpy as jnp
from jax import lax

F = 512
M = 128
SG = 512
TV = 128
TCAP = 16
FACETS = 16
TILES = 256


def draw_tile_count(key, part):
    keys = jax.random.split(key, 4)
    light = jax.random.randint(keys[0], (FACETS,), 1, max(2, TCAP // 4 + 1))
    heavy = jax.random.randint(keys[1], (FACETS,), max(1, TCAP // 2), TCAP + 1)
    chosen = jax.random.randint(keys[2], (FACETS,), 0, 8) == 0
    counts = jnp.where(chosen, heavy, light)
    fullest = jax.random.randint(keys[3], (), 0, FACETS)
    counts = jnp.where(jnp.arange(FACETS) == fullest, TCAP, counts)
    return counts.astype(jnp.int32)


def plant(array, key, smallest, high):
    longest = array.shape.index(max(array.shape))
    spots = []
    for shift in (0, 1):
        where = [jax.random.randint(jax.random.fold_in(key, axis), (), 0, length) for axis, length in enumerate(array.shape)]
        where[longest] = (where[longest] + shift) % array.shape[longest]
        spots.append(tuple(where))
    return array.at[spots[0]].set(smallest).at[spots[1]].set(high)


def shard_levels(key, extent, cuts, least, largest):
    level = 1.0
    for axis_at, parts in cuts:
        heights = jax.random.uniform(jax.random.fold_in(jax.random.fold_in(key, 6), axis_at), (parts,), jnp.float32, least / len(cuts), largest / len(cuts))
        level = level * jnp.repeat(jnp.exp(heights), extent[axis_at] // parts).reshape((-1,) + (1,) * (len(extent) - 1 - axis_at))
    return level


def scatter_about(rng, dims, scale, bound, cuts=(), kind=jnp.bfloat16):
    drawn = scale * jax.random.normal(rng, dims, jnp.float32)
    if cuts:
        drawn = drawn * shard_levels(rng, dims, cuts, -0.22, 0.18)
    return jnp.clip(drawn, -bound, bound).astype(kind)


def setup_inputs(seed: int = 0, part: int = 0) -> dict:
    key_list = jax.random.split(jax.random.key(seed), 8)
    part_splits = jax.random.split(jax.random.fold_in(key_list[7], part), 8)
    facets = scatter_about(part_splits[0], (FACETS, 2, F, F), 1.0, 6.0, ((0, 16),))
    facet_offsets = plant(jax.random.randint(part_splits[1], (FACETS, 2), 0, F), jax.random.fold_in(part_splits[1], 1), 0, F - 1).astype(jnp.int32)
    subgrid_offsets = plant(jax.random.randint(part_splits[2], (FACETS, 2), 0, F), jax.random.fold_in(part_splits[2], 1), 0, F - 1).astype(jnp.int32)
    w_terms = jnp.clip(jnp.exp(math.log(16.0) - 2.0794415 * jax.random.uniform(part_splits[3], (FACETS,), jnp.float32) ** shard_levels(part_splits[3], (FACETS,), ((0, 16),), -0.2, 0.2)), 2.0, 16.0)
    tile_count = draw_tile_count(jax.random.fold_in(jax.random.fold_in(key_list[7], part), 71), part)
    tile_offsets = plant(jax.random.randint(part_splits[5], (TILES, 2), 0, SG - 2 * TV + 1), jax.random.fold_in(part_splits[5], 1), 0, SG - 2 * TV).astype(jnp.int32)
    observed = scatter_about(part_splits[6], (TILES, 2, TV, TV), 1.0, 6.0, ((0, 16),))
    return {"facets": facets, "facet_offsets": facet_offsets, "subgrid_offsets": subgrid_offsets, "w_terms": w_terms, "tile_count": tile_count, "tile_offsets": tile_offsets, "observed": observed}


TWO_PI = 2.0 * math.pi

def basis_tables():
    index_f = jnp.arange(F, dtype=jnp.int32)
    product = index_f[:, None] * index_f[None, :] % F
    angle = -TWO_PI * product.astype(jnp.float32) / F
    scale = 1.0 / math.sqrt(F)
    return ((jnp.cos(angle) * scale).astype(jnp.bfloat16), (jnp.sin(angle) * scale).astype(jnp.bfloat16))

def padding_tables(facet_count):
    rows = jnp.arange(SG, dtype=jnp.int32)
    columns = jnp.arange(M, dtype=jnp.int32)
    product = rows[:, None] * columns[None, :] % SG
    angle = TWO_PI * product.astype(jnp.float32) / SG
    scale = (M * math.sqrt(facet_count)) ** (-0.5)
    return ((jnp.cos(angle) * scale).astype(jnp.bfloat16), (jnp.sin(angle) * scale).astype(jnp.bfloat16))

def taper_square():
    position = jnp.arange(M, dtype=jnp.float32)
    taper = 0.6 + 0.4 * jnp.sin(math.pi * (position + 0.5) / M)
    return taper[:, None] * taper[None, :]

def kernel_table():
    rows = jnp.arange(TV, dtype=jnp.float32)[:, None]
    columns = jnp.arange(2 * TV, dtype=jnp.float32)[None, :]
    distance = columns - 2.0 * rows - 1.0
    value = 0.75 * jnp.exp(-(distance / 1.5) * (distance / 1.5))
    return jnp.where(jnp.abs(distance) <= 4.0, value, jnp.zeros_like(value)).astype(jnp.bfloat16)

def facet_phase(offset):
    index_m = jnp.arange(M, dtype=jnp.int32)
    total = ((index_m * offset[0])[:, None] + (index_m * offset[1])[None, :]) % F
    angle = TWO_PI * total.astype(jnp.float32) / F
    return (jnp.cos(angle), jnp.sin(angle))

def screen_table(w_value):
    centred = jnp.arange(SG, dtype=jnp.float32) - SG / 2.0
    radius = (centred[:, None] * centred[:, None] + centred[None, :] * centred[None, :]) / (SG * SG)
    angle = TWO_PI * w_value * (jnp.sqrt(1.0 + radius) - 1.0)
    return (jnp.cos(angle), jnp.sin(angle))

def matmul(left, right):
    return jnp.dot(left, right, preferred_element_type=jnp.float32)

def complex_dot(left_real, left_imag, right_real, right_imag):
    real_part = matmul(left_real, right_real) - matmul(left_imag, right_imag)
    imag_part = matmul(left_real, right_imag) + matmul(left_imag, right_real)
    return (real_part, imag_part)

def facet_spectrum(facet, basis_real, basis_imag):
    half_real, half_imag = complex_dot(facet[0], facet[1], basis_real.T, basis_imag.T)
    return complex_dot(basis_real, basis_imag, half_real.astype(jnp.bfloat16), half_imag.astype(jnp.bfloat16))

def extract(spectrum_real, spectrum_imag, offsets, phase_cos, phase_sin, taper2):
    stacked = jnp.stack([spectrum_real, spectrum_imag])
    padded = jnp.concatenate([stacked, stacked[:, :M, :]], axis=1)
    padded = jnp.concatenate([padded, padded[:, :, :M]], axis=2)
    zero = jnp.zeros((), jnp.int32)

    def window(offset):
        return lax.dynamic_slice(padded, (zero, offset[0].astype(jnp.int32), offset[1].astype(jnp.int32)), (2, M, M))
    windows = jax.vmap(window)(offsets)
    real_part = taper2 * (phase_cos * windows[:, 0] - phase_sin * windows[:, 1])
    imag_part = taper2 * (phase_cos * windows[:, 1] + phase_sin * windows[:, 0])
    return jnp.stack([real_part, imag_part], axis=1).astype(jnp.bfloat16)

def subgrid_model(summed, pad_real, pad_imag, screen_cos, screen_sin):
    inner_real, inner_imag = complex_dot(pad_real, pad_imag, summed[0], summed[1])
    image_real, image_imag = complex_dot(inner_real.astype(jnp.bfloat16), inner_imag.astype(jnp.bfloat16), pad_real.T, pad_imag.T)
    model_real = screen_cos * image_real - screen_sin * image_imag
    model_imag = screen_cos * image_imag + screen_sin * image_real
    return jnp.stack([model_real, model_imag]).astype(jnp.bfloat16)

def tile_terms(model, observed_tile, offset, kernel):
    zero = jnp.zeros((), jnp.int32)
    window = lax.dynamic_slice(model, (zero, offset[0].astype(jnp.int32), offset[1].astype(jnp.int32)), (2, 2 * TV, 2 * TV))
    kernel32 = kernel.astype(jnp.float32)
    left = jnp.einsum('jq,cqk->cjk', kernel32, window.astype(jnp.float32)).astype(jnp.bfloat16)
    predicted = jnp.einsum('cjk,lk->cjl', left.astype(jnp.float32), kernel32)
    residual = (observed_tile.astype(jnp.float32) - predicted).astype(jnp.bfloat16)
    back = jnp.einsum('cjl,lk->cjk', residual.astype(jnp.float32), kernel32).astype(jnp.bfloat16)
    spread = jnp.einsum('jq,cjk->cqk', kernel32, back.astype(jnp.float32))
    return (residual, spread)

def add_window(adjoint, spread, offset):
    zero = jnp.zeros((), jnp.int32)
    start = (zero, offset[0].astype(jnp.int32), offset[1].astype(jnp.int32))
    current = lax.dynamic_slice(adjoint, start, spread.shape)
    return lax.dynamic_update_slice(adjoint, current + spread, start)

def back_coefficients(adjoint, pad_real, pad_imag, screen_cos, screen_sin):
    screened_real = (screen_cos * adjoint[0] + screen_sin * adjoint[1]).astype(jnp.bfloat16)
    screened_imag = (screen_cos * adjoint[1] - screen_sin * adjoint[0]).astype(jnp.bfloat16)
    reduced_real = (matmul(pad_real.T, screened_real) + matmul(pad_imag.T, screened_imag)).astype(jnp.bfloat16)
    reduced_imag = (matmul(pad_real.T, screened_imag) - matmul(pad_imag.T, screened_real)).astype(jnp.bfloat16)
    coef_real = matmul(reduced_real, pad_real) + matmul(reduced_imag, pad_imag)
    coef_imag = matmul(reduced_imag, pad_real) - matmul(reduced_real, pad_imag)
    return jnp.stack([coef_real, coef_imag]).astype(jnp.bfloat16)

def facet_back(back_spectrum, basis_real, basis_imag):
    half_real = (matmul(basis_real, back_spectrum[0]) + matmul(basis_imag, back_spectrum[1])).astype(jnp.bfloat16)
    half_imag = (matmul(basis_real, back_spectrum[1]) - matmul(basis_imag, back_spectrum[0])).astype(jnp.bfloat16)
    update_real = matmul(half_real, basis_real) + matmul(half_imag, basis_imag)
    update_imag = matmul(half_imag, basis_real) - matmul(half_real, basis_imag)
    return jnp.stack([update_real, update_imag]).astype(jnp.bfloat16)

def reference(facets, facet_offsets, subgrid_offsets, w_terms, tile_count, tile_offsets, observed):
    facet_count = facets.shape[0]
    basis_real, basis_imag = basis_tables()
    pad_real, pad_imag = padding_tables(facet_count)
    taper2 = taper_square()
    kernel = kernel_table()

    def forward_step(total, inputs):
        facet, offset = inputs
        spectrum_real, spectrum_imag = facet_spectrum(facet, basis_real, basis_imag)
        phase_cos, phase_sin = facet_phase(offset)
        contribution = extract(spectrum_real, spectrum_imag, subgrid_offsets, phase_cos, phase_sin, taper2)
        return (total + contribution.astype(jnp.float32), None)
    summed, _ = lax.scan(forward_step, jnp.zeros((facet_count, 2, M, M), jnp.float32), (facets, facet_offsets))
    observed_dev = observed.reshape(facet_count, TCAP, 2, TV, TV)
    offsets_dev = tile_offsets.reshape(facet_count, TCAP, 2)

    def subgrid_step(inputs):
        summed_one, w_value, count, tile_obs, tile_off = inputs
        screen_cos, screen_sin = screen_table(w_value)
        model = subgrid_model(summed_one.astype(jnp.bfloat16), pad_real, pad_imag, screen_cos, screen_sin)

        def tile_step(adjoint, tile_in):
            observed_tile, offset, slot = tile_in
            residual, spread = tile_terms(model, observed_tile, offset, kernel)
            live = slot < count
            residual = jnp.where(live, residual, jnp.zeros_like(residual))
            spread = jnp.where(live, spread, jnp.zeros_like(spread))
            return (add_window(adjoint, spread, offset), residual)
        adjoint, residuals = lax.scan(tile_step, jnp.zeros((2, SG, SG), jnp.float32), (tile_obs, tile_off, jnp.arange(TCAP, dtype=jnp.int32)))
        return (residuals, back_coefficients(adjoint, pad_real, pad_imag, screen_cos, screen_sin))
    residuals, coefficients = lax.map(subgrid_step, (summed, w_terms, tile_count, observed_dev, offsets_dev))
    index_m = jnp.arange(M, dtype=jnp.int32)
    row_index = (subgrid_offsets[:, 0:1] + index_m[None, :]) % F
    column_index = (subgrid_offsets[:, 1:2] + index_m[None, :]) % F
    coef32 = coefficients.astype(jnp.float32)

    def backward_step(offset):
        phase_cos, phase_sin = facet_phase(offset)
        values_real = taper2 * (phase_cos * coef32[:, 0] + phase_sin * coef32[:, 1])
        values_imag = taper2 * (phase_cos * coef32[:, 1] - phase_sin * coef32[:, 0])
        values = jnp.stack([values_real, values_imag])
        spectrum = jnp.zeros((2, F, F), jnp.float32).at[:, row_index[:, :, None], column_index[:, None, :]].add(values)
        return facet_back(spectrum.astype(jnp.bfloat16), basis_real, basis_imag)
    updates = lax.map(backward_step, facet_offsets)
    return (residuals.reshape(facet_count * TCAP, 2, TV, TV), updates)
```

```python
import functools
import math

import jax
import jax.numpy as jnp
import ml_dtypes
import numpy as np
from jax import lax
from jax.experimental import pallas as pl
from jax.experimental.pallas import tpu as pltpu
from jax.sharding import PartitionSpec as P

F = 512
M = 128
SG = 512
TV = 128
SPAN = 384
WIDE = F + M

BF16 = jnp.bfloat16
F32 = jnp.float32
TWO_PI = 2.0 * math.pi
MESH = pl.DeviceIdType.MESH
VMEM = pltpu.VMEM
LIMIT = 48 * 1024 * 1024


def basis_table():
    index = np.arange(F)
    angle = -TWO_PI * (index[:, None] * index[None, :] % F) / F
    scale = 1.0 / math.sqrt(F)
    return np.stack([np.cos(angle) * scale, np.sin(angle) * scale]).astype(ml_dtypes.bfloat16)


def padding_table(facet_count):
    angle = TWO_PI * (np.arange(SG)[:, None] * np.arange(M)[None, :] % SG) / SG
    scale = (M * math.sqrt(facet_count)) ** (-0.5)
    return np.stack([np.cos(angle) * scale, np.sin(angle) * scale]).astype(ml_dtypes.bfloat16)


def taper_square():
    taper = 0.6 + 0.4 * np.sin(math.pi * (np.arange(M) + 0.5) / M)
    return (taper[:, None] * taper[None, :]).astype(np.float32)


def kernel_table():
    distance = np.arange(2 * TV)[None, :] - 2.0 * np.arange(TV)[:, None] - 1.0
    value = 0.75 * np.exp(-(distance / 1.5) * (distance / 1.5))
    return np.where(np.abs(distance) <= 4.0, value, 0.0).astype(ml_dtypes.bfloat16).astype(np.float32)


def dot(left, right):
    return jnp.dot(left, right, preferred_element_type=F32)


def dot_t(left, right):
    return lax.dot_general(left, right, (((1,), (1,)), ((), ())), preferred_element_type=F32)


def cos_sin_turns(turns):
    quarter = jnp.floor(turns * 4.0 + 0.5)
    y = (turns - quarter * 0.25) * TWO_PI
    y2 = y * y
    sine = y * (1.0 + y2 * (-1.0 / 6 + y2 * (1.0 / 120 + y2 * (-1.0 / 5040 + y2 * (1.0 / 362880)))))
    cosine = 1.0 + y2 * (
        -0.5 + y2 * (1.0 / 24 + y2 * (-1.0 / 720 + y2 * (1.0 / 40320 - y2 * (1.0 / 3628800))))
    )
    which = quarter.astype(jnp.int32) & 3
    odd = (which & 1) == 1
    first = jnp.where(odd, sine, cosine)
    second = jnp.where(odd, cosine, sine)
    cos_value = jnp.where((which == 1) | (which == 2), -first, first)
    sin_value = jnp.where(which >= 2, -second, second)
    return cos_value, sin_value


def tapered_phase(offset_ref, taper_ref):
    rows = lax.broadcasted_iota(jnp.int32, (M, M), 0)
    columns = lax.broadcasted_iota(jnp.int32, (M, M), 1)
    total = (rows * offset_ref[0, 0] + columns * offset_ref[0, 1]) & (F - 1)
    cos_value, sin_value = cos_sin_turns(total.astype(F32) * (1.0 / F))
    taper = taper_ref[...]
    return cos_value * taper, sin_value * taper


def forward_kernel(n, foff, soff, facet, basis, taper, out, half, spec, phase):
    phase[0], phase[1] = tapered_phase(foff, taper)
    lanes = lax.broadcasted_iota(jnp.int32, (M, M), 1)

    @pl.loop(0, 2)
    def _(c):
        cols = pl.ds(pl.multiple_of(c * 256, 256), 256)
        br, bi = basis[0, :, cols], basis[1, :, cols]
        half[0, :, cols] = (dot(facet[0], br) - dot(facet[1], bi)).astype(BF16)
        half[1, :, cols] = (dot(facet[0], bi) + dot(facet[1], br)).astype(BF16)

    @pl.loop(0, 2)
    def _(c):
        cols = pl.ds(pl.multiple_of(c * 256, 256), 256)
        hr, hi = half[0, :, cols], half[1, :, cols]
        real = dot(basis[0], hr) - dot(basis[1], hi)
        imag = dot(basis[0], hi) + dot(basis[1], hr)
        for side in range(2):
            part = slice(side * M, side * M + M)
            spec[0, c * 2 + side, 0:F] = real[:, part]
            spec[1, c * 2 + side, 0:F] = imag[:, part]

    spec[:, 0 : F // M, F:WIDE] = spec[:, 0 : F // M, 0:M]
    spec[:, F // M] = spec[:, 0]

    @pl.loop(0, n)
    def _(s):
        sx, sy = soff[s, 0], soff[s, 1]
        tile, offset = sy >> 7, sy & 127
        shift = (M - offset) & 127
        kept = lanes < M - offset
        rows = pl.ds(sx, M)

        def window(plane):
            low = pltpu.roll(spec[plane, tile, rows], shift, 1)
            high = pltpu.roll(spec[plane, tile + 1, rows], shift, 1)
            return jnp.where(kept, low, high)

        real, imag = window(0), window(1)
        pc, ps = phase[0], phase[1]
        out[s & 1, s >> 1, 0] = (pc * real - ps * imag).astype(BF16)
        out[s & 1, s >> 1, 1] = (pc * imag + ps * real).astype(BF16)


def greet(me, chips, core):
    barrier = pltpu.get_barrier_semaphore()
    chip = me // 2
    for k in range(1, chips):
        pl.semaphore_signal(
            barrier, inc=1, device_id={"facet": lax.rem(chip + k, chips) * 2 + core}, device_id_type=MESH
        )
    pl.semaphore_signal(barrier, inc=1, device_id={"facet": chip * 2 + 1 - core}, device_id_type=MESH)
    pl.semaphore_wait(barrier, chips)


def reduce_kernel(chips, contrib, summed, near, pair, far, near_s, near_r, far_s, far_r):
    me = lax.axis_index("facet")
    chip, core = me // 2, lax.rem(me, 2)
    sibling = chip * 2 + 1 - core
    greet(me, chips, core)

    def near_copy(k):
        j = lax.rem(chip + k, chips)
        return pltpu.make_async_remote_copy(
            src_ref=contrib.at[1 - core, j],
            dst_ref=near.at[j],
            send_sem=near_s.at[j],
            recv_sem=near_r.at[j],
            device_id={"facet": sibling},
            device_id_type=MESH,
        )

    def far_send(k):
        j = lax.rem(chip + k, chips)
        return pltpu.make_async_remote_copy(
            src_ref=pair.at[j],
            dst_ref=far.at[chip],
            send_sem=far_s.at[j],
            recv_sem=far_r.at[chip],
            device_id={"facet": j * 2 + core},
            device_id_type=MESH,
        )

    def far_arrival(j):
        return pltpu.make_async_remote_copy(
            src_ref=pair.at[j],
            dst_ref=far.at[j],
            send_sem=far_s.at[j],
            recv_sem=far_r.at[j],
            device_id={"facet": j * 2 + core},
            device_id_type=MESH,
        )

    order = list(range(1, chips)) + [0]

    @pl.loop(1, chips + 1)
    def _(k):
        near_copy(k).start()

    @pl.loop(1, chips)
    def _(k):
        near_copy(k).wait_recv()
        j = lax.rem(chip + k, chips)
        pair[j] = (contrib[core, j].astype(F32) + near[j].astype(F32)).astype(BF16)
        far_send(k).start()

    near_copy(chips).wait_recv()
    summed[...] = contrib[core, chip].astype(F32) + near[chip].astype(F32)

    @pl.loop(1, chips)
    def _(k):
        j = lax.rem(chip + k, chips)
        far_arrival(j).wait_recv()
        summed[...] += far[j].astype(F32)

    @pl.loop(1, chips)
    def _(k):
        far_send(k).wait_send()

    @pl.loop(1, chips + 1)
    def _(k):
        near_copy(k).wait_send()


def gather_kernel(chips, mine, out, far_s, far_r, near_s, near_r, local):
    me = lax.axis_index("facet")
    chip, core = me // 2, lax.rem(me, 2)
    sibling = chip * 2 + 1 - core
    greet(me, chips, core)

    def far_send(k):
        j = lax.rem(chip + k, chips)
        return pltpu.make_async_remote_copy(
            src_ref=mine,
            dst_ref=out.at[me],
            send_sem=far_s.at[j],
            recv_sem=far_r.at[chip],
            device_id={"facet": j * 2 + core},
            device_id_type=MESH,
        )

    def far_arrival(j):
        return pltpu.make_async_remote_copy(
            src_ref=mine,
            dst_ref=out.at[j * 2 + core],
            send_sem=far_s.at[j],
            recv_sem=far_r.at[j],
            device_id={"facet": j * 2 + core},
            device_id_type=MESH,
        )

    def near_send(j):
        return pltpu.make_async_remote_copy(
            src_ref=out.at[j * 2 + core],
            dst_ref=out.at[j * 2 + core],
            send_sem=near_s.at[j],
            recv_sem=near_r.at[j],
            device_id={"facet": sibling},
            device_id_type=MESH,
        )

    def near_first():
        return pltpu.make_async_remote_copy(
            src_ref=mine,
            dst_ref=out.at[me],
            send_sem=near_s.at[chip],
            recv_sem=near_r.at[chip],
            device_id={"facet": sibling},
            device_id_type=MESH,
        )

    def near_arrival(j):
        return pltpu.make_async_remote_copy(
            src_ref=out.at[j * 2 + 1 - core],
            dst_ref=out.at[j * 2 + 1 - core],
            send_sem=near_s.at[j],
            recv_sem=near_r.at[j],
            device_id={"facet": sibling},
            device_id_type=MESH,
        )

    @pl.loop(1, chips)
    def _(k):
        far_send(k).start()

    near_first().start()
    own = pltpu.make_async_copy(mine, out.at[me], local)
    own.start()

    @pl.loop(1, chips)
    def _(k):
        j = lax.rem(chip + chips - k, chips)
        far_arrival(j).wait_recv()
        near_send(j).start()

    @pl.loop(0, chips)
    def _(k):
        near_arrival(lax.rem(chip + k, chips)).wait_recv()

    @pl.loop(1, chips)
    def _(k):
        far_send(k).wait_send()
        near_send(lax.rem(chip + k, chips)).wait_send()

    near_first().wait_send()
    own.wait()


def subgrid_kernel(
    slots, w_ref, count_ref, toff, summed, pad, pad_t, ker, ker_t, observed,
    residual, coefficient, inner, screen, model, adjoint, reduced, wide_t
):
    adjoint[...] = jnp.zeros_like(adjoint)
    residual[...] = jnp.zeros_like(residual)
    wide_t[...] = ker_t[...]
    sr, si = summed[0].astype(BF16), summed[1].astype(BF16)
    inner[0] = (dot(pad[0], sr) - dot(pad[1], si)).astype(BF16)
    inner[1] = (dot(pad[0], si) + dot(pad[1], sr)).astype(BF16)
    w_value = w_ref[0]

    @pl.loop(0, 4)
    def _(c):
        rows = pl.ds(pl.multiple_of(c * 128, 128), 128)
        u = (lax.broadcasted_iota(jnp.int32, (128, SG), 0) + (c * 128 - 256)).astype(F32)
        v = (lax.broadcasted_iota(jnp.int32, (128, SG), 1) - 256).astype(F32)
        radius = (u * u + v * v) * (1.0 / (SG * SG))
        cos_value, sin_value = cos_sin_turns(w_value * (jnp.sqrt(1.0 + radius) - 1.0))
        screen[0, rows, :] = cos_value
        screen[1, rows, :] = sin_value
        ir, ii = inner[0, rows, :], inner[1, rows, :]
        image_real = dot(ir, pad_t[0]) - dot(ii, pad_t[1])
        image_imag = dot(ir, pad_t[1]) + dot(ii, pad_t[0])
        model[0, rows, :] = (cos_value * image_real - sin_value * image_imag).astype(BF16)
        model[1, rows, :] = (cos_value * image_imag + sin_value * image_real).astype(BF16)

    count = count_ref[0]

    @pl.loop(0, count)
    def _(t):
        ou, ov = toff[t, 0], toff[t, 1]
        u0 = pl.multiple_of(jnp.minimum(ou & ~127, 128), 128)
        v0 = pl.multiple_of(jnp.minimum(ov & ~127, 128), 128)
        du, dv = ou - u0, ov - v0
        rows, cols = pl.ds(u0, SPAN), pl.ds(v0, SPAN)
        table = ker[...]
        ku = pltpu.roll(table, du, 1).astype(BF16)
        kv = pltpu.roll(table, dv, 1).astype(BF16)
        kut = wide_t[pl.ds(128 - du, SPAN), :].astype(BF16)
        left = jnp.concatenate(
            [dot(ku, model[0, rows, cols]).astype(BF16), dot(ku, model[1, rows, cols]).astype(BF16)], axis=0
        )
        predicted = dot_t(left, kv)
        seen = observed[t].reshape(2 * TV, TV).astype(F32)
        rest = (seen - predicted).astype(BF16)
        residual[t] = rest.reshape(2, TV, TV)
        back = dot(rest, kv).astype(BF16)
        adjoint[0, rows, cols] += dot(kut, back[:TV])
        adjoint[1, rows, cols] += dot(kut, back[TV:])

    reduced[...] = jnp.zeros_like(reduced)

    @pl.loop(0, 2)
    def _(c):
        cols = pl.ds(pl.multiple_of(c * 256, 256), 256)
        ar, ai = adjoint[0, :, cols], adjoint[1, :, cols]
        sc, ss = screen[0, :, cols], screen[1, :, cols]
        xr = (sc * ar + ss * ai).astype(BF16)
        xi = (sc * ai - ss * ar).astype(BF16)
        reduced[0, :, cols] = (dot(pad_t[0], xr) + dot(pad_t[1], xi)).astype(BF16)
        reduced[1, :, cols] = (dot(pad_t[0], xi) - dot(pad_t[1], xr)).astype(BF16)

    rr, ri = reduced[0], reduced[1]
    coefficient[0] = (dot(rr, pad[0]) + dot(ri, pad[1])).astype(BF16)
    coefficient[1] = (dot(ri, pad[0]) - dot(rr, pad[1])).astype(BF16)


def backward_kernel(n, foff, soff, piece, basis, taper, out, acc, spec, half, phase):
    phase[0], phase[1] = tapered_phase(foff, taper)
    lanes = lax.broadcasted_iota(jnp.int32, (M, M), 1)
    acc[...] = jnp.zeros_like(acc)

    @pl.loop(0, n)
    def _(s):
        sx, sy = soff[s, 0], soff[s, 1]
        tile, shift = sy >> 7, sy & 127
        rows = pl.ds(sx, M)
        kept = lanes >= shift
        pc, ps = phase[0], phase[1]
        real, imag = piece[s, 0].astype(F32), piece[s, 1].astype(F32)
        blank = jnp.zeros((M, M), F32)
        values = (pc * real + ps * imag, pc * imag - ps * real)
        for plane in range(2):
            turned = pltpu.roll(values[plane], shift, 1)
            acc[plane, tile, rows] += jnp.where(kept, turned, blank)
            acc[plane, tile + 1, rows] += jnp.where(kept, blank, turned)

    acc[:, 0] += acc[:, F // M]
    acc[:, 0 : F // M, 0:M] += acc[:, 0 : F // M, F:WIDE]
    for k in range(F // M):
        spec[:, :, k * M : k * M + M] = acc[:, k, 0:F].astype(BF16)

    @pl.loop(0, 2)
    def _(c):
        cols = pl.ds(pl.multiple_of(c * 256, 256), 256)
        xr, xi = spec[0, :, cols], spec[1, :, cols]
        half[0, :, cols] = (dot(basis[0], xr) + dot(basis[1], xi)).astype(BF16)
        half[1, :, cols] = (dot(basis[0], xi) - dot(basis[1], xr)).astype(BF16)

    @pl.loop(0, 2)
    def _(c):
        cols = pl.ds(pl.multiple_of(c * 256, 256), 256)
        br, bi = basis[0, :, cols], basis[1, :, cols]
        out[0, :, cols] = (dot(half[0], br) + dot(half[1], bi)).astype(BF16)
        out[1, :, cols] = (dot(half[1], br) - dot(half[0], bi)).astype(BF16)


SMEM_SPEC = pl.BlockSpec(memory_space=pltpu.SMEM)
VMEM_SPEC = pl.BlockSpec(memory_space=pltpu.VMEM)
DMA = pltpu.SemaphoreType.DMA


def per_device(facets, facet_offsets, subgrid_offsets, w_terms, tile_count, tile_offsets, observed):
    n = lax.axis_size("facet")
    chips = n // 2
    slots = observed.shape[0]
    basis = jnp.asarray(basis_table())
    pad_np = padding_table(n)
    pad = jnp.asarray(pad_np)
    pad_t = jnp.asarray(np.ascontiguousarray(pad_np.transpose(0, 2, 1)))
    taper = jnp.asarray(taper_square())
    table = kernel_table()
    ker_np = np.zeros((TV, SPAN), np.float32)
    ker_np[:, : 2 * TV] = table
    ker_t_np = np.zeros((4 * TV, TV), np.float32)
    ker_t_np[TV : 3 * TV] = table.T
    plain = pltpu.CompilerParams(vmem_limit_bytes=LIMIT)

    contrib = pl.pallas_call(
        functools.partial(forward_kernel, n),
        out_shape=jax.ShapeDtypeStruct((2, chips, 2, M, M), BF16),
        in_specs=[SMEM_SPEC, SMEM_SPEC, VMEM_SPEC, VMEM_SPEC, VMEM_SPEC],
        out_specs=VMEM_SPEC,
        scratch_shapes=[
            VMEM((2, F, F), BF16), VMEM((2, WIDE // M, WIDE, M), F32), VMEM((2, M, M), F32),
        ],
        compiler_params=plain,
        name="forward",
    )(facet_offsets, subgrid_offsets, facets[0], basis, taper)

    summed = pl.pallas_call(
        functools.partial(reduce_kernel, chips),
        out_shape=jax.ShapeDtypeStruct((2, M, M), F32),
        in_specs=[VMEM_SPEC],
        out_specs=VMEM_SPEC,
        scratch_shapes=[VMEM((chips, 2, M, M), BF16)] * 3 + [DMA((chips,))] * 4,
        compiler_params=pltpu.CompilerParams(
            vmem_limit_bytes=LIMIT, collective_id=0, has_side_effects=True
        ),
        name="reduce",
    )(contrib)

    residual, coefficient = pl.pallas_call(
        functools.partial(subgrid_kernel, slots),
        out_shape=(
            jax.ShapeDtypeStruct((slots, 2, TV, TV), BF16),
            jax.ShapeDtypeStruct((2, M, M), BF16),
        ),
        in_specs=[SMEM_SPEC] * 3 + [VMEM_SPEC] * 6,
        out_specs=(VMEM_SPEC, VMEM_SPEC),
        scratch_shapes=[
            VMEM((2, SG, M), BF16), VMEM((2, SG, SG), F32), VMEM((2, SG, SG), BF16),
            VMEM((2, SG, SG), F32), VMEM((2, M, SG), BF16), VMEM((4 * TV, TV), F32),
        ],
        compiler_params=plain,
        name="subgrid",
    )(
        w_terms, tile_count, tile_offsets, summed, pad, pad_t,
        jnp.asarray(ker_np), jnp.asarray(ker_t_np), observed,
    )

    piece = pl.pallas_call(
        functools.partial(gather_kernel, chips),
        out_shape=jax.ShapeDtypeStruct((n, 2, M, M), BF16),
        in_specs=[VMEM_SPEC],
        out_specs=VMEM_SPEC,
        scratch_shapes=[DMA((chips,))] * 4 + [DMA],
        compiler_params=pltpu.CompilerParams(
            vmem_limit_bytes=LIMIT, collective_id=1, has_side_effects=True
        ),
        name="gather",
    )(coefficient)

    update = pl.pallas_call(
        functools.partial(backward_kernel, n),
        out_shape=jax.ShapeDtypeStruct((2, F, F), BF16),
        in_specs=[SMEM_SPEC, SMEM_SPEC, VMEM_SPEC, VMEM_SPEC, VMEM_SPEC],
        out_specs=VMEM_SPEC,
        scratch_shapes=[
            VMEM((2, WIDE // M, WIDE, M), F32), VMEM((2, F, F), BF16), VMEM((2, F, F), BF16),
            VMEM((2, M, M), F32),
        ],
        compiler_params=plain,
        name="backward",
    )(facet_offsets, subgrid_offsets, piece, basis, taper)
    return (residual, update[None])


def solution(mesh):
    placed = (
        P(("groups", "facet"), None, None, None),
        P(("groups", "facet"), None),
        P("groups", None),
        P(("groups", "facet")),
        P(("groups", "facet")),
        P(("groups", "facet"), None),
        P(("groups", "facet"), None, None, None),
    )
    return jax.shard_map(
        per_device,
        mesh=mesh,
        in_specs=placed,
        out_specs=(
            P(("groups", "facet"), None, None, None),
            P(("groups", "facet"), None, None, None),
        ),
        check_vma=False,
    )
```

```python
import functools
import math

import jax
import jax.numpy as jnp
import ml_dtypes
import numpy as np
from jax import lax
from jax.experimental import pallas as pl
from jax.experimental.pallas import tpu as pltpu
from jax.sharding import PartitionSpec as P

F = 512
M = 128
SG = 512
TV = 128
SPAN = 384
WIDE = F + M
GROUP = 2

BF16 = jnp.bfloat16
F32 = jnp.float32
TWO_PI = 2.0 * math.pi
MESH = pl.DeviceIdType.MESH
VMEM = pltpu.VMEM
LIMIT = 48 * 1024 * 1024


def basis_table():
    index = np.arange(F)
    angle = -TWO_PI * (index[:, None] * index[None, :] % F) / F
    scale = 1.0 / math.sqrt(F)
    return np.stack([np.cos(angle) * scale, np.sin(angle) * scale]).astype(ml_dtypes.bfloat16)


def padding_table(facet_count):
    angle = TWO_PI * (np.arange(SG)[:, None] * np.arange(M)[None, :] % SG) / SG
    scale = (M * math.sqrt(facet_count)) ** (-0.5)
    return np.stack([np.cos(angle) * scale, np.sin(angle) * scale]).astype(ml_dtypes.bfloat16)


def taper_square():
    taper = 0.6 + 0.4 * np.sin(math.pi * (np.arange(M) + 0.5) / M)
    return (taper[:, None] * taper[None, :]).astype(np.float32)


def kernel_table():
    distance = np.arange(2 * TV)[None, :] - 2.0 * np.arange(TV)[:, None] - 1.0
    value = 0.75 * np.exp(-(distance / 1.5) * (distance / 1.5))
    return np.where(np.abs(distance) <= 4.0, value, 0.0).astype(ml_dtypes.bfloat16).astype(np.float32)


def dot(left, right):
    return jnp.dot(left, right, preferred_element_type=F32)


def dot_t(left, right):
    return lax.dot_general(left, right, (((1,), (1,)), ((), ())), preferred_element_type=F32)


def cos_sin_turns(turns):
    quarter = jnp.floor(turns * 4.0 + 0.5)
    y = (turns - quarter * 0.25) * TWO_PI
    y2 = y * y
    sine = y * (1.0 + y2 * (-1.0 / 6 + y2 * (1.0 / 120 + y2 * (-1.0 / 5040 + y2 * (1.0 / 362880)))))
    cosine = 1.0 + y2 * (
        -0.5 + y2 * (1.0 / 24 + y2 * (-1.0 / 720 + y2 * (1.0 / 40320 - y2 * (1.0 / 3628800))))
    )
    which = quarter.astype(jnp.int32) & 3
    odd = (which & 1) == 1
    first = jnp.where(odd, sine, cosine)
    second = jnp.where(odd, cosine, sine)
    cos_value = jnp.where((which == 1) | (which == 2), -first, first)
    sin_value = jnp.where(which >= 2, -second, second)
    return cos_value, sin_value


def tapered_phase(offset_ref, taper_ref):
    rows = lax.broadcasted_iota(jnp.int32, (M, M), 0)
    columns = lax.broadcasted_iota(jnp.int32, (M, M), 1)
    total = (rows * offset_ref[0, 0] + columns * offset_ref[0, 1]) & (F - 1)
    cos_value, sin_value = cos_sin_turns(total.astype(F32) * (1.0 / F))
    taper = taper_ref[...]
    return cos_value * taper, sin_value * taper


def forward_kernel(
    n, foff_h, soff_h, facet_h, basis_h, taper_h, out,
    half, spec, phase, foff, soff, facet, basis, taper, sems
):
    pairs = ((facet_h, facet), (basis_h, basis), (taper_h, taper), (foff_h, foff), (soff_h, soff))
    copies = [pltpu.make_async_copy(src, dst, sems.at[i]) for i, (src, dst) in enumerate(pairs)]
    for copy in copies:
        copy.start()
    for copy in copies:
        copy.wait()
    phase[0], phase[1] = tapered_phase(foff, taper)
    lanes = lax.broadcasted_iota(jnp.int32, (M, M), 1)

    @pl.loop(0, 2)
    def _(c):
        cols = pl.ds(pl.multiple_of(c * 256, 256), 256)
        br, bi = basis[0, :, cols], basis[1, :, cols]
        half[0, :, cols] = (dot(facet[0], br) - dot(facet[1], bi)).astype(BF16)
        half[1, :, cols] = (dot(facet[0], bi) + dot(facet[1], br)).astype(BF16)

    @pl.loop(0, 2)
    def _(c):
        cols = pl.ds(pl.multiple_of(c * 256, 256), 256)
        hr, hi = half[0, :, cols], half[1, :, cols]
        real = dot(basis[0], hr) - dot(basis[1], hi)
        imag = dot(basis[0], hi) + dot(basis[1], hr)
        for side in range(2):
            part = slice(side * M, side * M + M)
            spec[0, c * 2 + side, 0:F] = real[:, part]
            spec[1, c * 2 + side, 0:F] = imag[:, part]

    spec[:, 0 : F // M, F:WIDE] = spec[:, 0 : F // M, 0:M]
    spec[:, F // M] = spec[:, 0]

    @pl.loop(0, n)
    def _(s):
        sx, sy = soff[0, s], soff[1, s]
        tile, offset = sy >> 7, sy & 127
        shift = (M - offset) & 127
        kept = lanes < M - offset
        rows = pl.ds(sx, M)

        def window(plane):
            low = pltpu.roll(spec[plane, tile, rows], shift, 1)
            high = pltpu.roll(spec[plane, tile + 1, rows], shift, 1)
            return jnp.where(kept, low, high)

        real, imag = window(0), window(1)
        pc, ps = phase[0], phase[1]
        out[s & 1, s >> 1, 0] = (pc * real - ps * imag).astype(BF16)
        out[s & 1, s >> 1, 1] = (pc * imag + ps * real).astype(BF16)


def greet(me, chips, core):
    barrier = pltpu.get_barrier_semaphore()
    chip = me // 2
    for k in range(1, chips):
        pl.semaphore_signal(
            barrier, inc=1, device_id={"facet": lax.rem(chip + k, chips) * 2 + core}, device_id_type=MESH
        )
    pl.semaphore_signal(barrier, inc=1, device_id={"facet": chip * 2 + 1 - core}, device_id_type=MESH)
    pl.semaphore_wait(barrier, chips)


def reduce_kernel(chips, contrib, summed, near, pair, far, near_s, near_r, far_s, far_r):
    me = lax.axis_index("facet")
    chip, core = me // 2, lax.rem(me, 2)
    sibling = chip * 2 + 1 - core
    greet(me, chips, core)

    def near_copy(k):
        j = lax.rem(chip + k, chips)
        return pltpu.make_async_remote_copy(
            src_ref=contrib.at[1 - core, j],
            dst_ref=near.at[j],
            send_sem=near_s.at[j],
            recv_sem=near_r.at[j],
            device_id={"facet": sibling},
            device_id_type=MESH,
        )

    def far_send(k):
        j = lax.rem(chip + k, chips)
        return pltpu.make_async_remote_copy(
            src_ref=pair.at[j],
            dst_ref=far.at[chip],
            send_sem=far_s.at[j],
            recv_sem=far_r.at[chip],
            device_id={"facet": j * 2 + core},
            device_id_type=MESH,
        )

    def far_arrival(j):
        return pltpu.make_async_remote_copy(
            src_ref=pair.at[j],
            dst_ref=far.at[j],
            send_sem=far_s.at[j],
            recv_sem=far_r.at[j],
            device_id={"facet": j * 2 + core},
            device_id_type=MESH,
        )

    order = list(range(1, chips)) + [0]

    @pl.loop(1, chips + 1)
    def _(k):
        near_copy(k).start()

    @pl.loop(1, chips)
    def _(k):
        near_copy(k).wait_recv()
        j = lax.rem(chip + k, chips)
        pair[j] = (contrib[core, j].astype(F32) + near[j].astype(F32)).astype(BF16)
        far_send(k).start()

    near_copy(chips).wait_recv()
    summed[...] = contrib[core, chip].astype(F32) + near[chip].astype(F32)

    @pl.loop(1, chips)
    def _(k):
        j = lax.rem(chip + k, chips)
        far_arrival(j).wait_recv()
        summed[...] += far[j].astype(F32)

    @pl.loop(1, chips)
    def _(k):
        far_send(k).wait_send()

    @pl.loop(1, chips + 1)
    def _(k):
        near_copy(k).wait_send()


def gather_kernel(chips, mine, out, far_s, far_r, near_s, near_r, local):
    me = lax.axis_index("facet")
    chip, core = me // 2, lax.rem(me, 2)
    sibling = chip * 2 + 1 - core
    greet(me, chips, core)

    def far_send(k):
        j = lax.rem(chip + k, chips)
        return pltpu.make_async_remote_copy(
            src_ref=mine,
            dst_ref=out.at[me],
            send_sem=far_s.at[j],
            recv_sem=far_r.at[chip],
            device_id={"facet": j * 2 + core},
            device_id_type=MESH,
        )

    def far_arrival(j):
        return pltpu.make_async_remote_copy(
            src_ref=mine,
            dst_ref=out.at[j * 2 + core],
            send_sem=far_s.at[j],
            recv_sem=far_r.at[j],
            device_id={"facet": j * 2 + core},
            device_id_type=MESH,
        )

    def near_send(j):
        return pltpu.make_async_remote_copy(
            src_ref=out.at[j * 2 + core],
            dst_ref=out.at[j * 2 + core],
            send_sem=near_s.at[j],
            recv_sem=near_r.at[j],
            device_id={"facet": sibling},
            device_id_type=MESH,
        )

    def near_first():
        return pltpu.make_async_remote_copy(
            src_ref=mine,
            dst_ref=out.at[me],
            send_sem=near_s.at[chip],
            recv_sem=near_r.at[chip],
            device_id={"facet": sibling},
            device_id_type=MESH,
        )

    def near_arrival(j):
        return pltpu.make_async_remote_copy(
            src_ref=out.at[j * 2 + 1 - core],
            dst_ref=out.at[j * 2 + 1 - core],
            send_sem=near_s.at[j],
            recv_sem=near_r.at[j],
            device_id={"facet": sibling},
            device_id_type=MESH,
        )

    @pl.loop(1, chips)
    def _(k):
        far_send(k).start()

    near_first().start()
    own = pltpu.make_async_copy(mine, out.at[me], local)
    own.start()

    @pl.loop(1, chips)
    def _(k):
        j = lax.rem(chip + chips - k, chips)
        far_arrival(j).wait_recv()
        near_send(j).start()

    @pl.loop(0, chips)
    def _(k):
        near_arrival(lax.rem(chip + k, chips)).wait_recv()

    @pl.loop(1, chips)
    def _(k):
        far_send(k).wait_send()
        near_send(lax.rem(chip + k, chips)).wait_send()

    near_first().wait_send()
    own.wait()


def subgrid_kernel(
    slots, w_ref, count_ref, toff, summed, pad, pad_t, ker, ker_t, observed,
    residual, coefficient, inner, screen, model, adjoint, reduced, wide_t
):
    adjoint[...] = jnp.zeros_like(adjoint)
    residual[...] = jnp.zeros_like(residual)
    wide_t[...] = ker_t[...]
    sr, si = summed[0].astype(BF16), summed[1].astype(BF16)
    inner[0] = (dot(pad[0], sr) - dot(pad[1], si)).astype(BF16)
    inner[1] = (dot(pad[0], si) + dot(pad[1], sr)).astype(BF16)
    w_value = w_ref[0]

    @pl.loop(0, 4)
    def _(c):
        rows = pl.ds(pl.multiple_of(c * 128, 128), 128)
        u = (lax.broadcasted_iota(jnp.int32, (128, SG), 0) + (c * 128 - 256)).astype(F32)
        v = (lax.broadcasted_iota(jnp.int32, (128, SG), 1) - 256).astype(F32)
        radius = (u * u + v * v) * (1.0 / (SG * SG))
        cos_value, sin_value = cos_sin_turns(w_value * (jnp.sqrt(1.0 + radius) - 1.0))
        screen[0, rows, :] = cos_value
        screen[1, rows, :] = sin_value
        ir, ii = inner[0, rows, :], inner[1, rows, :]
        image_real = dot(ir, pad_t[0]) - dot(ii, pad_t[1])
        image_imag = dot(ir, pad_t[1]) + dot(ii, pad_t[0])
        model[0, rows, :] = (cos_value * image_real - sin_value * image_imag).astype(BF16)
        model[1, rows, :] = (cos_value * image_imag + sin_value * image_real).astype(BF16)

    count = count_ref[0]

    lanes = lax.broadcasted_iota(jnp.int32, (TV, TV), 1)
    blank = jnp.zeros((TV, TV), F32)

    def shifted(amount):
        low = pltpu.roll(ker[:, :TV], amount & 127, 1)
        high = pltpu.roll(ker[:, TV : 2 * TV], amount & 127, 1)
        inside = lanes >= amount
        return jnp.concatenate(
            [
                jnp.where(inside, low, blank).astype(BF16),
                jnp.where(inside, high, low).astype(BF16),
                jnp.where(inside, blank, high).astype(BF16),
            ],
            axis=1,
        )

    @pl.loop(0, (count + GROUP - 1) // GROUP)
    def _(step):
        slot = [step * GROUP + g for g in range(GROUP)]
        spans, ku, kv, kut = [], [], [], []
        for t in slot:
            ou, ov = toff[0, t], toff[1, t]
            u0 = pl.multiple_of(jnp.minimum(ou & ~127, 128), 128)
            v0 = pl.multiple_of(jnp.minimum(ov & ~127, 128), 128)
            spans.append((pl.ds(u0, SPAN), pl.ds(v0, SPAN)))
            ku.append(shifted(ou - u0))
            kv.append(shifted(ov - v0))
            kut.append(wide_t[pl.ds(128 - (ou - u0), SPAN), :].astype(BF16))
        left = [
            jnp.concatenate(
                [dot(ku[g], model[p, spans[g][0], spans[g][1]]).astype(BF16) for p in range(2)], axis=0
            )
            for g in range(GROUP)
        ]
        predicted = [dot_t(left[g], kv[g]) for g in range(GROUP)]
        rest = []
        for g, t in enumerate(slot):
            seen = observed[t].reshape(2 * TV, TV).astype(F32)
            value = (seen - predicted[g]).astype(BF16)
            rest.append(jnp.where(t < count, value, jnp.zeros_like(value)))
            residual[t] = rest[g].reshape(2, TV, TV)
        back = [dot(rest[g], kv[g]).astype(BF16) for g in range(GROUP)]
        spread = [[dot(kut[g], back[g][p * TV : p * TV + TV]) for p in range(2)] for g in range(GROUP)]
        for g in range(GROUP):
            for p in range(2):
                adjoint[p, spans[g][0], spans[g][1]] += spread[g][p]

    @pl.loop(0, 2)
    def _(c):
        cols = pl.ds(pl.multiple_of(c * 256, 256), 256)
        ar, ai = adjoint[0, :, cols], adjoint[1, :, cols]
        sc, ss = screen[0, :, cols], screen[1, :, cols]
        xr = (sc * ar + ss * ai).astype(BF16)
        xi = (sc * ai - ss * ar).astype(BF16)
        reduced[0, :, cols] = (dot(pad_t[0], xr) + dot(pad_t[1], xi)).astype(BF16)
        reduced[1, :, cols] = (dot(pad_t[0], xi) - dot(pad_t[1], xr)).astype(BF16)

    rr, ri = reduced[0], reduced[1]
    coefficient[0] = (dot(rr, pad[0]) + dot(ri, pad[1])).astype(BF16)
    coefficient[1] = (dot(ri, pad[0]) - dot(rr, pad[1])).astype(BF16)


def backward_kernel(n, foff, soff, piece, basis, taper, out, acc, spec, half, phase):
    phase[0], phase[1] = tapered_phase(foff, taper)
    lanes = lax.broadcasted_iota(jnp.int32, (M, M), 1)
    acc[...] = jnp.zeros_like(acc)

    @pl.loop(0, n)
    def _(s):
        sx, sy = soff[0, s], soff[1, s]
        tile, shift = sy >> 7, sy & 127
        rows = pl.ds(sx, M)
        kept = lanes >= shift
        pc, ps = phase[0], phase[1]
        real, imag = piece[s, 0].astype(F32), piece[s, 1].astype(F32)
        blank = jnp.zeros((M, M), F32)
        values = (pc * real + ps * imag, pc * imag - ps * real)
        for plane in range(2):
            turned = pltpu.roll(values[plane], shift, 1)
            acc[plane, tile, rows] += jnp.where(kept, turned, blank)
            acc[plane, tile + 1, rows] += jnp.where(kept, blank, turned)

    acc[:, 0] += acc[:, F // M]
    acc[:, 0 : F // M, 0:M] += acc[:, 0 : F // M, F:WIDE]
    for k in range(F // M):
        spec[:, :, k * M : k * M + M] = acc[:, k, 0:F].astype(BF16)

    @pl.loop(0, 2)
    def _(c):
        cols = pl.ds(pl.multiple_of(c * 256, 256), 256)
        xr, xi = spec[0, :, cols], spec[1, :, cols]
        half[0, :, cols] = (dot(basis[0], xr) + dot(basis[1], xi)).astype(BF16)
        half[1, :, cols] = (dot(basis[0], xi) - dot(basis[1], xr)).astype(BF16)

    @pl.loop(0, 2)
    def _(c):
        cols = pl.ds(pl.multiple_of(c * 256, 256), 256)
        br, bi = basis[0, :, cols], basis[1, :, cols]
        out[0, :, cols] = (dot(half[0], br) + dot(half[1], bi)).astype(BF16)
        out[1, :, cols] = (dot(half[1], br) - dot(half[0], bi)).astype(BF16)


SMEM_SPEC = pl.BlockSpec(memory_space=pltpu.SMEM)
VMEM_SPEC = pl.BlockSpec(memory_space=pltpu.VMEM)
HBM_SPEC = pl.BlockSpec(memory_space=pltpu.HBM)
DMA = pltpu.SemaphoreType.DMA


def per_device(facets, facet_offsets, subgrid_offsets, w_terms, tile_count, tile_offsets, observed):
    n = lax.axis_size("facet")
    chips = n // 2
    soff_t = subgrid_offsets.T
    slots = observed.shape[0]
    basis = jnp.asarray(basis_table())
    pad_np = padding_table(n)
    pad = jnp.asarray(pad_np)
    pad_t = jnp.asarray(np.ascontiguousarray(pad_np.transpose(0, 2, 1)))
    taper = jnp.asarray(taper_square())
    table = kernel_table()
    ker_t_np = np.zeros((4 * TV, TV), np.float32)
    ker_t_np[TV : 3 * TV] = table.T
    plain = pltpu.CompilerParams(vmem_limit_bytes=LIMIT)

    contrib = pl.pallas_call(
        functools.partial(forward_kernel, n),
        out_shape=jax.ShapeDtypeStruct((2, chips, 2, M, M), BF16),
        in_specs=[HBM_SPEC] * 5,
        out_specs=VMEM_SPEC,
        scratch_shapes=[
            VMEM((2, F, F), BF16), VMEM((2, WIDE // M, WIDE, M), F32), VMEM((2, M, M), F32),
            pltpu.SMEM((1, 2), jnp.int32), pltpu.SMEM((2, n), jnp.int32),
            VMEM((2, F, F), BF16), VMEM((2, F, F), BF16), VMEM((M, M), F32), DMA((5,)),
        ],
        compiler_params=plain,
        name="forward",
    )(facet_offsets, soff_t, facets[0], basis, taper)

    summed = pl.pallas_call(
        functools.partial(reduce_kernel, chips),
        out_shape=jax.ShapeDtypeStruct((2, M, M), F32),
        in_specs=[VMEM_SPEC],
        out_specs=VMEM_SPEC,
        scratch_shapes=[VMEM((chips, 2, M, M), BF16)] * 3 + [DMA((chips,))] * 4,
        compiler_params=pltpu.CompilerParams(
            vmem_limit_bytes=LIMIT, collective_id=0, has_side_effects=True
        ),
        name="reduce",
    )(contrib)

    residual, coefficient = pl.pallas_call(
        functools.partial(subgrid_kernel, slots),
        out_shape=(
            jax.ShapeDtypeStruct((slots, 2, TV, TV), BF16),
            jax.ShapeDtypeStruct((2, M, M), BF16),
        ),
        in_specs=[SMEM_SPEC] * 3 + [VMEM_SPEC] * 6,
        out_specs=(VMEM_SPEC, VMEM_SPEC),
        scratch_shapes=[
            VMEM((2, SG, M), BF16), VMEM((2, SG, SG), F32), VMEM((2, SG, SG), BF16),
            VMEM((2, SG, SG), F32), VMEM((2, M, SG), BF16), VMEM((4 * TV, TV), F32),
        ],
        compiler_params=plain,
        name="subgrid",
    )(
        w_terms, tile_count, tile_offsets.T, summed, pad, pad_t,
        jnp.asarray(table), jnp.asarray(ker_t_np), observed,
    )

    piece = pl.pallas_call(
        functools.partial(gather_kernel, chips),
        out_shape=jax.ShapeDtypeStruct((n, 2, M, M), BF16),
        in_specs=[VMEM_SPEC],
        out_specs=VMEM_SPEC,
        scratch_shapes=[DMA((chips,))] * 4 + [DMA],
        compiler_params=pltpu.CompilerParams(
            vmem_limit_bytes=LIMIT, collective_id=1, has_side_effects=True
        ),
        name="gather",
    )(coefficient)

    update = pl.pallas_call(
        functools.partial(backward_kernel, n),
        out_shape=jax.ShapeDtypeStruct((2, F, F), BF16),
        in_specs=[SMEM_SPEC, SMEM_SPEC, VMEM_SPEC, VMEM_SPEC, VMEM_SPEC],
        out_specs=VMEM_SPEC,
        scratch_shapes=[
            VMEM((2, WIDE // M, WIDE, M), F32), VMEM((2, F, F), BF16), VMEM((2, F, F), BF16),
            VMEM((2, M, M), F32),
        ],
        compiler_params=plain,
        name="backward",
    )(facet_offsets, soff_t, piece, basis, taper)
    return (residual, update[None])


def solution(mesh):
    placed = (
        P(("groups", "facet"), None, None, None),
        P(("groups", "facet"), None),
        P("groups", None),
        P(("groups", "facet")),
        P(("groups", "facet")),
        P(("groups", "facet"), None),
        P(("groups", "facet"), None, None, None),
    )
    return jax.shard_map(
        per_device,
        mesh=mesh,
        in_specs=placed,
        out_specs=(
            P(("groups", "facet"), None, None, None),
            P(("groups", "facet"), None, None, None),
        ),
        check_vma=False,
    )
```

```python
import functools
import math

import jax
import jax.numpy as jnp
import ml_dtypes
import numpy as np
from jax import lax
from jax.experimental import pallas as pl
from jax.experimental.pallas import tpu as pltpu
from jax.sharding import PartitionSpec as P

F = 512
M = 128
SG = 512
TV = 128
SPAN = 384
WIDE = F + M
GROUP = 2

BF16 = jnp.bfloat16
F32 = jnp.float32
TWO_PI = 2.0 * math.pi
MESH = pl.DeviceIdType.MESH
VMEM = pltpu.VMEM
LIMIT = 48 * 1024 * 1024


def basis_table():
    index = np.arange(F)
    angle = -TWO_PI * (index[:, None] * index[None, :] % F) / F
    scale = 1.0 / math.sqrt(F)
    return np.stack([np.cos(angle) * scale, np.sin(angle) * scale]).astype(ml_dtypes.bfloat16)


def padding_table(facet_count):
    angle = TWO_PI * (np.arange(SG)[:, None] * np.arange(M)[None, :] % SG) / SG
    scale = (M * math.sqrt(facet_count)) ** (-0.5)
    return np.stack([np.cos(angle) * scale, np.sin(angle) * scale]).astype(ml_dtypes.bfloat16)


def taper_square():
    taper = 0.6 + 0.4 * np.sin(math.pi * (np.arange(M) + 0.5) / M)
    return (taper[:, None] * taper[None, :]).astype(np.float32)


def kernel_table():
    distance = np.arange(2 * TV)[None, :] - 2.0 * np.arange(TV)[:, None] - 1.0
    value = 0.75 * np.exp(-(distance / 1.5) * (distance / 1.5))
    return np.where(np.abs(distance) <= 4.0, value, 0.0).astype(ml_dtypes.bfloat16).astype(np.float32)


def dot(left, right):
    return jnp.dot(left, right, preferred_element_type=F32)


def dot_t(left, right):
    return lax.dot_general(left, right, (((1,), (1,)), ((), ())), preferred_element_type=F32)


def cos_sin_turns(turns):
    quarter = jnp.floor(turns * 4.0 + 0.5)
    y = (turns - quarter * 0.25) * TWO_PI
    y2 = y * y
    sine = y * (1.0 + y2 * (-1.0 / 6 + y2 * (1.0 / 120 + y2 * (-1.0 / 5040 + y2 * (1.0 / 362880)))))
    cosine = 1.0 + y2 * (
        -0.5 + y2 * (1.0 / 24 + y2 * (-1.0 / 720 + y2 * (1.0 / 40320 - y2 * (1.0 / 3628800))))
    )
    which = quarter.astype(jnp.int32) & 3
    odd = (which & 1) == 1
    first = jnp.where(odd, sine, cosine)
    second = jnp.where(odd, cosine, sine)
    cos_value = jnp.where((which == 1) | (which == 2), -first, first)
    sin_value = jnp.where(which >= 2, -second, second)
    return cos_value, sin_value


def tapered_phase(offset_ref, taper_ref):
    rows = lax.broadcasted_iota(jnp.int32, (M, M), 0)
    columns = lax.broadcasted_iota(jnp.int32, (M, M), 1)
    total = (rows * offset_ref[0, 0] + columns * offset_ref[0, 1]) & (F - 1)
    cos_value, sin_value = cos_sin_turns(total.astype(F32) * (1.0 / F))
    taper = taper_ref[...]
    return cos_value * taper, sin_value * taper


def forward_kernel(
    n, foff_h, soff_h, facet_h, basis_h, taper_h, out,
    half, spec, phase, foff, soff, facet, basis, taper, sems
):
    pairs = ((facet_h, facet), (basis_h, basis), (taper_h, taper), (foff_h, foff), (soff_h, soff))
    copies = [pltpu.make_async_copy(src, dst, sems.at[i]) for i, (src, dst) in enumerate(pairs)]
    for copy in copies:
        copy.start()
    for copy in copies:
        copy.wait()
    phase[0], phase[1] = tapered_phase(foff, taper)
    lanes = lax.broadcasted_iota(jnp.int32, (M, M), 1)

    @pl.loop(0, 2)
    def _(c):
        cols = pl.ds(pl.multiple_of(c * 256, 256), 256)
        br, bi = basis[0, :, cols], basis[1, :, cols]
        half[0, :, cols] = (dot(facet[0], br) - dot(facet[1], bi)).astype(BF16)
        half[1, :, cols] = (dot(facet[0], bi) + dot(facet[1], br)).astype(BF16)

    @pl.loop(0, 2)
    def _(c):
        cols = pl.ds(pl.multiple_of(c * 256, 256), 256)
        hr, hi = half[0, :, cols], half[1, :, cols]
        real = dot(basis[0], hr) - dot(basis[1], hi)
        imag = dot(basis[0], hi) + dot(basis[1], hr)
        for side in range(2):
            part = slice(side * M, side * M + M)
            spec[0, c * 2 + side, 0:F] = real[:, part]
            spec[1, c * 2 + side, 0:F] = imag[:, part]

    spec[:, 0 : F // M, F:WIDE] = spec[:, 0 : F // M, 0:M]
    spec[:, F // M] = spec[:, 0]

    @pl.loop(0, n)
    def _(s):
        sx, sy = soff[0, s], soff[1, s]
        tile, offset = sy >> 7, sy & 127
        shift = (M - offset) & 127
        kept = lanes < M - offset
        rows = pl.ds(sx, M)

        def window(plane):
            low = pltpu.roll(spec[plane, tile, rows], shift, 1)
            high = pltpu.roll(spec[plane, tile + 1, rows], shift, 1)
            return jnp.where(kept, low, high)

        real, imag = window(0), window(1)
        pc, ps = phase[0], phase[1]
        out[s & 1, (s >> 1) & 1, s >> 2, 0] = (pc * real - ps * imag).astype(BF16)
        out[s & 1, (s >> 1) & 1, s >> 2, 1] = (pc * imag + ps * real).astype(BF16)


def place(n):
    me = lax.axis_index("facet")
    quads = n // 4
    far_first = [1 + (t + quads // 2 - 1) % (quads - 1) for t in range(quads - 1)]
    return quads, me // 4, lax.rem(me // 2, 2), lax.rem(me, 2), far_first


def index(quad, middle, core):
    return quad * 4 + middle * 2 + core


def greet(peers):
    barrier = pltpu.get_barrier_semaphore()
    for peer in peers:
        pl.semaphore_signal(barrier, inc=1, device_id={"facet": peer}, device_id_type=MESH)
    pl.semaphore_wait(barrier, len(peers))


def send(src, dst, send_sem, recv_sem, peer):
    return pltpu.make_async_remote_copy(
        src_ref=src, dst_ref=dst, send_sem=send_sem, recv_sem=recv_sem,
        device_id={"facet": peer}, device_id_type=MESH,
    )


def reduce_kernel(
    n, contrib, summed, near, pair, mid, quad_sum, far,
    near_s, near_r, mid_s, mid_r, far_s, far_r
):
    quads, quad, middle, core, far_first = place(n)
    other = 1 - middle
    sibling, beside = index(quad, middle, 1 - core), index(quad, other, core)
    away = [lax.rem(quad + k, quads) for k in far_first]
    order = away + [quad]
    greet([index(j, middle, core) for j in away] + [beside, sibling])

    def near_copy(half, j):
        return send(contrib.at[1 - core, half, j], near.at[half, j], near_s.at[half, j], near_r.at[half, j], sibling)

    def mid_copy(j):
        return send(pair.at[j], mid.at[j], mid_s.at[j], mid_r.at[j], beside)

    def far_copy(j, slot):
        return send(quad_sum.at[j], far.at[slot], far_s.at[j], far_r.at[slot], index(j, middle, core))

    def near_sum(half, j):
        return contrib[core, half, j].astype(F32) + near[half, j].astype(F32)

    for half in (other, middle):
        for j in order:
            near_copy(half, j).start()
    for j in order:
        near_copy(other, j).wait_recv()
        pair[j] = near_sum(other, j).astype(BF16)
        mid_copy(j).start()
    for j in away:
        near_copy(middle, j).wait_recv()
        mid_copy(j).wait_recv()
        quad_sum[j] = (near_sum(middle, j) + mid[j].astype(F32)).astype(BF16)
        far_copy(j, quad).start()
    near_copy(middle, quad).wait_recv()
    mid_copy(quad).wait_recv()
    total = near_sum(middle, quad) + mid[quad].astype(F32)
    for j in reversed(away):
        far_copy(j, j).wait_recv()
        total = total + far[j].astype(F32)
    summed[...] = total
    for j in order:
        near_copy(other, j).wait_send()
        near_copy(middle, j).wait_send()
        mid_copy(j).wait_send()
    for j in away:
        far_copy(j, quad).wait_send()


def gather_kernel(n, mine, out, near_s, near_r, mid_s, mid_r, far_s, far_r, local):
    quads, quad, middle, core, far_first = place(n)
    other = 1 - middle
    me = index(quad, middle, core)
    sibling, beside = index(quad, middle, 1 - core), index(quad, other, core)
    away = [lax.rem(quad + k, quads) for k in far_first]
    back = [lax.rem(quad + quads - k, quads) for k in far_first]
    greet([index(j, middle, core) for j in away] + [beside, sibling])

    def far_copy(j, slot):
        return send(
            mine, out.at[index(slot, middle, core)], far_s.at[j], far_r.at[slot], index(j, middle, core)
        )

    def mid_copy(j, half):
        piece = out.at[index(j, half, core)]
        return send(piece, piece, mid_s.at[j], mid_r.at[j], beside)

    def near_copy(half, j, side):
        piece = out.at[index(j, half, side)]
        return send(piece, piece, near_s.at[half, j], near_r.at[half, j], sibling)

    for j in away:
        far_copy(j, quad).start()
    mid_own = send(mine, out.at[me], mid_s.at[quad], mid_r.at[quad], beside)
    mid_own.start()
    near_own = send(mine, out.at[me], near_s.at[middle, quad], near_r.at[middle, quad], sibling)
    near_own.start()
    own = pltpu.make_async_copy(mine, out.at[me], local)
    own.start()
    for j in back:
        far_copy(j, j).wait_recv()
        mid_copy(j, middle).start()
        near_copy(middle, j, core).start()
    for j in [quad] + back:
        mid_copy(j, other).wait_recv()
        near_copy(other, j, core).start()
    for half in (middle, other):
        for j in [quad] + back:
            near_copy(half, j, 1 - core).wait_recv()
    for j in away:
        far_copy(j, quad).wait_send()
        mid_copy(j, middle).wait_send()
        near_copy(middle, j, core).wait_send()
        near_copy(other, j, core).wait_send()
    near_copy(other, quad, core).wait_send()
    mid_own.wait_send()
    near_own.wait_send()
    own.wait()


def subgrid_kernel(
    slots, w_ref, count_ref, toff, summed, pad, pad_t, ker, ker_t, observed,
    residual, coefficient, inner, screen, model, adjoint, reduced, wide_t
):
    adjoint[...] = jnp.zeros_like(adjoint)
    residual[...] = jnp.zeros_like(residual)
    wide_t[...] = ker_t[...]
    sr, si = summed[0].astype(BF16), summed[1].astype(BF16)
    inner[0] = (dot(pad[0], sr) - dot(pad[1], si)).astype(BF16)
    inner[1] = (dot(pad[0], si) + dot(pad[1], sr)).astype(BF16)
    w_value = w_ref[0]

    @pl.loop(0, 4)
    def _(c):
        rows = pl.ds(pl.multiple_of(c * 128, 128), 128)
        u = (lax.broadcasted_iota(jnp.int32, (128, SG), 0) + (c * 128 - 256)).astype(F32)
        v = (lax.broadcasted_iota(jnp.int32, (128, SG), 1) - 256).astype(F32)
        radius = (u * u + v * v) * (1.0 / (SG * SG))
        cos_value, sin_value = cos_sin_turns(w_value * (jnp.sqrt(1.0 + radius) - 1.0))
        screen[0, rows, :] = cos_value
        screen[1, rows, :] = sin_value
        ir, ii = inner[0, rows, :], inner[1, rows, :]
        image_real = dot(ir, pad_t[0]) - dot(ii, pad_t[1])
        image_imag = dot(ir, pad_t[1]) + dot(ii, pad_t[0])
        model[0, rows, :] = (cos_value * image_real - sin_value * image_imag).astype(BF16)
        model[1, rows, :] = (cos_value * image_imag + sin_value * image_real).astype(BF16)

    count = count_ref[0]

    lanes = lax.broadcasted_iota(jnp.int32, (TV, TV), 1)
    blank = jnp.zeros((TV, TV), F32)

    def shifted(amount):
        low = pltpu.roll(ker[:, :TV], amount & 127, 1)
        high = pltpu.roll(ker[:, TV : 2 * TV], amount & 127, 1)
        inside = lanes >= amount
        return jnp.concatenate(
            [
                jnp.where(inside, low, blank).astype(BF16),
                jnp.where(inside, high, low).astype(BF16),
                jnp.where(inside, blank, high).astype(BF16),
            ],
            axis=1,
        )

    @pl.loop(0, (count + GROUP - 1) // GROUP)
    def _(step):
        slot = [step * GROUP + g for g in range(GROUP)]
        spans, ku, kv, kut = [], [], [], []
        for t in slot:
            ou, ov = toff[0, t], toff[1, t]
            u0 = pl.multiple_of(jnp.minimum(ou & ~127, 128), 128)
            v0 = pl.multiple_of(jnp.minimum(ov & ~127, 128), 128)
            spans.append((pl.ds(u0, SPAN), pl.ds(v0, SPAN)))
            ku.append(shifted(ou - u0))
            kv.append(shifted(ov - v0))
            kut.append(wide_t[pl.ds(128 - (ou - u0), SPAN), :].astype(BF16))
        left = [
            jnp.concatenate(
                [dot(ku[g], model[p, spans[g][0], spans[g][1]]).astype(BF16) for p in range(2)], axis=0
            )
            for g in range(GROUP)
        ]
        predicted = [dot_t(left[g], kv[g]) for g in range(GROUP)]
        rest = []
        for g, t in enumerate(slot):
            seen = observed[t].reshape(2 * TV, TV).astype(F32)
            value = (seen - predicted[g]).astype(BF16)
            rest.append(jnp.where(t < count, value, jnp.zeros_like(value)))
            residual[t] = rest[g].reshape(2, TV, TV)
        back = [dot(rest[g], kv[g]).astype(BF16) for g in range(GROUP)]
        spread = [[dot(kut[g], back[g][p * TV : p * TV + TV]) for p in range(2)] for g in range(GROUP)]
        for g in range(GROUP):
            for p in range(2):
                adjoint[p, spans[g][0], spans[g][1]] += spread[g][p]

    @pl.loop(0, 2)
    def _(c):
        cols = pl.ds(pl.multiple_of(c * 256, 256), 256)
        ar, ai = adjoint[0, :, cols], adjoint[1, :, cols]
        sc, ss = screen[0, :, cols], screen[1, :, cols]
        xr = (sc * ar + ss * ai).astype(BF16)
        xi = (sc * ai - ss * ar).astype(BF16)
        reduced[0, :, cols] = (dot(pad_t[0], xr) + dot(pad_t[1], xi)).astype(BF16)
        reduced[1, :, cols] = (dot(pad_t[0], xi) - dot(pad_t[1], xr)).astype(BF16)

    rr, ri = reduced[0], reduced[1]
    coefficient[0] = (dot(rr, pad[0]) + dot(ri, pad[1])).astype(BF16)
    coefficient[1] = (dot(ri, pad[0]) - dot(rr, pad[1])).astype(BF16)


def backward_kernel(n, foff, soff, piece, basis, taper, out, acc, spec, half, phase):
    phase[0], phase[1] = tapered_phase(foff, taper)
    lanes = lax.broadcasted_iota(jnp.int32, (M, M), 1)
    acc[...] = jnp.zeros_like(acc)

    @pl.loop(0, n)
    def _(s):
        sx, sy = soff[0, s], soff[1, s]
        tile, shift = sy >> 7, sy & 127
        rows = pl.ds(sx, M)
        kept = lanes >= shift
        pc, ps = phase[0], phase[1]
        real, imag = piece[s, 0].astype(F32), piece[s, 1].astype(F32)
        blank = jnp.zeros((M, M), F32)
        values = (pc * real + ps * imag, pc * imag - ps * real)
        for plane in range(2):
            turned = pltpu.roll(values[plane], shift, 1)
            acc[plane, tile, rows] += jnp.where(kept, turned, blank)
            acc[plane, tile + 1, rows] += jnp.where(kept, blank, turned)

    acc[:, 0] += acc[:, F // M]
    acc[:, 0 : F // M, 0:M] += acc[:, 0 : F // M, F:WIDE]
    for k in range(F // M):
        spec[:, :, k * M : k * M + M] = acc[:, k, 0:F].astype(BF16)

    @pl.loop(0, 2)
    def _(c):
        cols = pl.ds(pl.multiple_of(c * 256, 256), 256)
        xr, xi = spec[0, :, cols], spec[1, :, cols]
        half[0, :, cols] = (dot(basis[0], xr) + dot(basis[1], xi)).astype(BF16)
        half[1, :, cols] = (dot(basis[0], xi) - dot(basis[1], xr)).astype(BF16)

    @pl.loop(0, 2)
    def _(c):
        cols = pl.ds(pl.multiple_of(c * 256, 256), 256)
        br, bi = basis[0, :, cols], basis[1, :, cols]
        out[0, :, cols] = (dot(half[0], br) + dot(half[1], bi)).astype(BF16)
        out[1, :, cols] = (dot(half[1], br) - dot(half[0], bi)).astype(BF16)


SMEM_SPEC = pl.BlockSpec(memory_space=pltpu.SMEM)
VMEM_SPEC = pl.BlockSpec(memory_space=pltpu.VMEM)
HBM_SPEC = pl.BlockSpec(memory_space=pltpu.HBM)
DMA = pltpu.SemaphoreType.DMA


def per_device(facets, facet_offsets, subgrid_offsets, w_terms, tile_count, tile_offsets, observed):
    n = lax.axis_size("facet")
    quads = n // 4
    soff_t = subgrid_offsets.T
    slots = observed.shape[0]
    basis = jnp.asarray(basis_table())
    pad_np = padding_table(n)
    pad = jnp.asarray(pad_np)
    pad_t = jnp.asarray(np.ascontiguousarray(pad_np.transpose(0, 2, 1)))
    taper = jnp.asarray(taper_square())
    table = kernel_table()
    ker_t_np = np.zeros((4 * TV, TV), np.float32)
    ker_t_np[TV : 3 * TV] = table.T
    plain = pltpu.CompilerParams(vmem_limit_bytes=LIMIT)

    contrib = pl.pallas_call(
        functools.partial(forward_kernel, n),
        out_shape=jax.ShapeDtypeStruct((2, 2, quads, 2, M, M), BF16),
        in_specs=[HBM_SPEC] * 5,
        out_specs=VMEM_SPEC,
        scratch_shapes=[
            VMEM((2, F, F), BF16), VMEM((2, WIDE // M, WIDE, M), F32), VMEM((2, M, M), F32),
            pltpu.SMEM((1, 2), jnp.int32), pltpu.SMEM((2, n), jnp.int32),
            VMEM((2, F, F), BF16), VMEM((2, F, F), BF16), VMEM((M, M), F32), DMA((5,)),
        ],
        compiler_params=plain,
        name="forward",
    )(*[pltpu.with_memory_space_constraint(x, pltpu.HBM) for x in (facet_offsets, soff_t, facets[0], basis, taper)])

    summed = pl.pallas_call(
        functools.partial(reduce_kernel, n),
        out_shape=jax.ShapeDtypeStruct((2, M, M), F32),
        in_specs=[VMEM_SPEC],
        out_specs=VMEM_SPEC,
        scratch_shapes=[VMEM((2, quads, 2, M, M), BF16)]
        + [VMEM((quads, 2, M, M), BF16)] * 4
        + [DMA((2, quads))] * 2
        + [DMA((quads,))] * 4,
        compiler_params=pltpu.CompilerParams(
            vmem_limit_bytes=LIMIT, collective_id=0, has_side_effects=True
        ),
        name="reduce",
    )(contrib)

    residual, coefficient = pl.pallas_call(
        functools.partial(subgrid_kernel, slots),
        out_shape=(
            jax.ShapeDtypeStruct((slots, 2, TV, TV), BF16),
            jax.ShapeDtypeStruct((2, M, M), BF16),
        ),
        in_specs=[SMEM_SPEC] * 3 + [VMEM_SPEC] * 6,
        out_specs=(VMEM_SPEC, VMEM_SPEC),
        scratch_shapes=[
            VMEM((2, SG, M), BF16), VMEM((2, SG, SG), F32), VMEM((2, SG, SG), BF16),
            VMEM((2, SG, SG), F32), VMEM((2, M, SG), BF16), VMEM((4 * TV, TV), F32),
        ],
        compiler_params=plain,
        name="subgrid",
    )(
        w_terms, tile_count, tile_offsets.T, summed, pad, pad_t,
        jnp.asarray(table), jnp.asarray(ker_t_np), observed,
    )

    piece = pl.pallas_call(
        functools.partial(gather_kernel, n),
        out_shape=jax.ShapeDtypeStruct((n, 2, M, M), BF16),
        in_specs=[VMEM_SPEC],
        out_specs=VMEM_SPEC,
        scratch_shapes=[DMA((2, quads))] * 2 + [DMA((quads,))] * 4 + [DMA],
        compiler_params=pltpu.CompilerParams(
            vmem_limit_bytes=LIMIT, collective_id=1, has_side_effects=True
        ),
        name="gather",
    )(coefficient)

    update = pl.pallas_call(
        functools.partial(backward_kernel, n),
        out_shape=jax.ShapeDtypeStruct((2, F, F), BF16),
        in_specs=[SMEM_SPEC, SMEM_SPEC, VMEM_SPEC, VMEM_SPEC, VMEM_SPEC],
        out_specs=VMEM_SPEC,
        scratch_shapes=[
            VMEM((2, WIDE // M, WIDE, M), F32), VMEM((2, F, F), BF16), VMEM((2, F, F), BF16),
            VMEM((2, M, M), F32),
        ],
        compiler_params=plain,
        name="backward",
    )(facet_offsets, soff_t, piece, basis, taper)
    return (residual, update[None])


def solution(mesh):
    placed = (
        P(("groups", "facet"), None, None, None),
        P(("groups", "facet"), None),
        P("groups", None),
        P(("groups", "facet")),
        P(("groups", "facet")),
        P(("groups", "facet"), None),
        P(("groups", "facet"), None, None, None),
    )
    return jax.shard_map(
        per_device,
        mesh=mesh,
        in_specs=placed,
        out_specs=(
            P(("groups", "facet"), None, None, None),
            P(("groups", "facet"), None, None, None),
        ),
        check_vma=False,
    )
```

```python
import functools
import math

import jax
import jax.numpy as jnp
import ml_dtypes
import numpy as np
from jax import lax
from jax.experimental import pallas as pl
from jax.experimental.pallas import tpu as pltpu
from jax.sharding import PartitionSpec as P

F = 512
M = 128
SG = 512
TV = 128
SPAN = 384
WIDE = F + M
GROUP = 4

BF16 = jnp.bfloat16
F32 = jnp.float32
TWO_PI = 2.0 * math.pi
MESH = pl.DeviceIdType.MESH
VMEM = pltpu.VMEM
LIMIT = 48 * 1024 * 1024


def basis_table():
    index = np.arange(F)
    angle = -TWO_PI * (index[:, None] * index[None, :] % F) / F
    scale = 1.0 / math.sqrt(F)
    return np.stack([np.cos(angle) * scale, np.sin(angle) * scale]).astype(ml_dtypes.bfloat16)


def padding_table(facet_count):
    angle = TWO_PI * (np.arange(SG)[:, None] * np.arange(M)[None, :] % SG) / SG
    scale = (M * math.sqrt(facet_count)) ** (-0.5)
    return np.stack([np.cos(angle) * scale, np.sin(angle) * scale]).astype(ml_dtypes.bfloat16)


def taper_square():
    taper = 0.6 + 0.4 * np.sin(math.pi * (np.arange(M) + 0.5) / M)
    return (taper[:, None] * taper[None, :]).astype(np.float32)


def kernel_table():
    distance = np.arange(2 * TV)[None, :] - 2.0 * np.arange(TV)[:, None] - 1.0
    value = 0.75 * np.exp(-(distance / 1.5) * (distance / 1.5))
    return np.where(np.abs(distance) <= 4.0, value, 0.0).astype(ml_dtypes.bfloat16).astype(np.float32)


def dot(left, right):
    return jnp.dot(left, right, preferred_element_type=F32)


def dot_t(left, right):
    return lax.dot_general(left, right, (((1,), (1,)), ((), ())), preferred_element_type=F32)


def cos_sin_turns(turns):
    quarter = jnp.floor(turns * 4.0 + 0.5)
    y = (turns - quarter * 0.25) * TWO_PI
    y2 = y * y
    sine = y * (1.0 + y2 * (-1.0 / 6 + y2 * (1.0 / 120 + y2 * (-1.0 / 5040 + y2 * (1.0 / 362880)))))
    cosine = 1.0 + y2 * (
        -0.5 + y2 * (1.0 / 24 + y2 * (-1.0 / 720 + y2 * (1.0 / 40320 - y2 * (1.0 / 3628800))))
    )
    which = quarter.astype(jnp.int32) & 3
    odd = (which & 1) == 1
    first = jnp.where(odd, sine, cosine)
    second = jnp.where(odd, cosine, sine)
    cos_value = jnp.where((which == 1) | (which == 2), -first, first)
    sin_value = jnp.where(which >= 2, -second, second)
    return cos_value, sin_value


def tapered_phase(offset_ref, taper_ref):
    rows = lax.broadcasted_iota(jnp.int32, (M, M), 0)
    columns = lax.broadcasted_iota(jnp.int32, (M, M), 1)
    total = (rows * offset_ref[0, 0] + columns * offset_ref[0, 1]) & (F - 1)
    cos_value, sin_value = cos_sin_turns(total.astype(F32) * (1.0 / F))
    taper = taper_ref[...]
    return cos_value * taper, sin_value * taper


def forward_kernel(
    n, foff_h, soff_h, facet_h, basis_h, taper_h, out,
    half, spec, phase, foff, soff, facet, basis, taper, sems
):
    pairs = ((facet_h, facet), (basis_h, basis), (taper_h, taper), (foff_h, foff), (soff_h, soff))
    copies = [pltpu.make_async_copy(src, dst, sems.at[i]) for i, (src, dst) in enumerate(pairs)]
    for copy in copies:
        copy.start()
    for copy in copies:
        copy.wait()
    phase[0], phase[1] = tapered_phase(foff, taper)
    lanes = lax.broadcasted_iota(jnp.int32, (M, M), 1)

    @pl.loop(0, 2)
    def _(c):
        cols = pl.ds(pl.multiple_of(c * 256, 256), 256)
        br, bi = basis[0, :, cols], basis[1, :, cols]
        half[0, :, cols] = (dot(facet[0], br) - dot(facet[1], bi)).astype(BF16)
        half[1, :, cols] = (dot(facet[0], bi) + dot(facet[1], br)).astype(BF16)

    @pl.loop(0, 2)
    def _(c):
        cols = pl.ds(pl.multiple_of(c * 256, 256), 256)
        hr, hi = half[0, :, cols], half[1, :, cols]
        real = dot(basis[0], hr) - dot(basis[1], hi)
        imag = dot(basis[0], hi) + dot(basis[1], hr)
        for side in range(2):
            part = slice(side * M, side * M + M)
            spec[0, c * 2 + side, 0:F] = real[:, part]
            spec[1, c * 2 + side, 0:F] = imag[:, part]

    spec[:, 0 : F // M, F:WIDE] = spec[:, 0 : F // M, 0:M]
    spec[:, F // M] = spec[:, 0]

    @pl.loop(0, n)
    def _(s):
        sx, sy = soff[0, s], soff[1, s]
        tile, offset = sy >> 7, sy & 127
        shift = (M - offset) & 127
        kept = lanes < M - offset
        rows = pl.ds(sx, M)

        def window(plane):
            low = pltpu.roll(spec[plane, tile, rows], shift, 1)
            high = pltpu.roll(spec[plane, tile + 1, rows], shift, 1)
            return jnp.where(kept, low, high)

        real, imag = window(0), window(1)
        pc, ps = phase[0], phase[1]
        out[s & 1, (s >> 1) & 1, s >> 2, 0] = (pc * real - ps * imag).astype(BF16)
        out[s & 1, (s >> 1) & 1, s >> 2, 1] = (pc * imag + ps * real).astype(BF16)


def place(n):
    me = lax.axis_index("facet")
    quads = n // 4
    far_first = [1 + (t + quads // 2 - 1) % (quads - 1) for t in range(quads - 1)]
    return quads, me // 4, lax.rem(me // 2, 2), lax.rem(me, 2), far_first


def index(quad, middle, core):
    return quad * 4 + middle * 2 + core


def greet(peers):
    barrier = pltpu.get_barrier_semaphore()
    for peer in peers:
        pl.semaphore_signal(barrier, inc=1, device_id={"facet": peer}, device_id_type=MESH)
    pl.semaphore_wait(barrier, len(peers))


def send(src, dst, send_sem, recv_sem, peer):
    return pltpu.make_async_remote_copy(
        src_ref=src, dst_ref=dst, send_sem=send_sem, recv_sem=recv_sem,
        device_id={"facet": peer}, device_id_type=MESH,
    )


def fill_screen(w_value, screen):
    @pl.loop(0, 4)
    def _(c):
        rows = pl.ds(pl.multiple_of(c * 128, 128), 128)
        u = (lax.broadcasted_iota(jnp.int32, (128, SG), 0) + (c * 128 - 256)).astype(F32)
        v = (lax.broadcasted_iota(jnp.int32, (128, SG), 1) - 256).astype(F32)
        radius = (u * u + v * v) * (1.0 / (SG * SG))
        cos_value, sin_value = cos_sin_turns(w_value * (jnp.sqrt(1.0 + radius) - 1.0))
        screen[0, rows, :] = cos_value
        screen[1, rows, :] = sin_value


def reduce_kernel(
    n, w_ref, contrib, summed, screen, near, pair, mid, quad_sum, far,
    near_s, near_r, mid_s, mid_r, far_s, far_r
):
    quads, quad, middle, core, far_first = place(n)
    other = 1 - middle
    sibling, beside = index(quad, middle, 1 - core), index(quad, other, core)
    away = [lax.rem(quad + k, quads) for k in far_first]
    order = away + [quad]
    greet([index(j, middle, core) for j in away] + [beside, sibling])

    def near_copy(half, j):
        return send(contrib.at[1 - core, half, j], near.at[half, j], near_s.at[half, j], near_r.at[half, j], sibling)

    def mid_copy(j):
        return send(pair.at[j], mid.at[j], mid_s.at[j], mid_r.at[j], beside)

    def far_copy(j, slot):
        return send(quad_sum.at[j], far.at[slot], far_s.at[j], far_r.at[slot], index(j, middle, core))

    def near_sum(half, j):
        return contrib[core, half, j].astype(F32) + near[half, j].astype(F32)

    for half in (other, middle):
        for j in order:
            near_copy(half, j).start()
    for j in order:
        near_copy(other, j).wait_recv()
        pair[j] = near_sum(other, j).astype(BF16)
        mid_copy(j).start()
    for j in away:
        near_copy(middle, j).wait_recv()
        mid_copy(j).wait_recv()
        quad_sum[j] = (near_sum(middle, j) + mid[j].astype(F32)).astype(BF16)
        far_copy(j, quad).start()
    fill_screen(w_ref[0], screen)
    near_copy(middle, quad).wait_recv()
    mid_copy(quad).wait_recv()
    total = near_sum(middle, quad) + mid[quad].astype(F32)
    for j in reversed(away):
        far_copy(j, j).wait_recv()
        total = total + far[j].astype(F32)
    summed[...] = total
    for j in order:
        near_copy(other, j).wait_send()
        near_copy(middle, j).wait_send()
        mid_copy(j).wait_send()
    for j in away:
        far_copy(j, quad).wait_send()


def gather_kernel(n, mine, out, near_s, near_r, mid_s, mid_r, far_s, far_r, local):
    quads, quad, middle, core, far_first = place(n)
    other = 1 - middle
    me = index(quad, middle, core)
    sibling, beside = index(quad, middle, 1 - core), index(quad, other, core)
    away = [lax.rem(quad + k, quads) for k in far_first]
    back = [lax.rem(quad + quads - k, quads) for k in far_first]
    greet([index(j, middle, core) for j in away] + [beside, sibling])

    def far_copy(j, slot):
        return send(
            mine, out.at[index(slot, middle, core)], far_s.at[j], far_r.at[slot], index(j, middle, core)
        )

    def mid_copy(j, half):
        piece = out.at[index(j, half, core)]
        return send(piece, piece, mid_s.at[j], mid_r.at[j], beside)

    def near_copy(half, j, side):
        piece = out.at[index(j, half, side)]
        return send(piece, piece, near_s.at[half, j], near_r.at[half, j], sibling)

    for j in away:
        far_copy(j, quad).start()
    mid_own = send(mine, out.at[me], mid_s.at[quad], mid_r.at[quad], beside)
    mid_own.start()
    near_own = send(mine, out.at[me], near_s.at[middle, quad], near_r.at[middle, quad], sibling)
    near_own.start()
    own = pltpu.make_async_copy(mine, out.at[me], local)
    own.start()
    for j in back:
        far_copy(j, j).wait_recv()
        mid_copy(j, middle).start()
        near_copy(middle, j, core).start()
    for j in [quad] + back:
        mid_copy(j, other).wait_recv()
        near_copy(other, j, core).start()
    for half in (middle, other):
        for j in [quad] + back:
            near_copy(half, j, 1 - core).wait_recv()
    for j in away:
        far_copy(j, quad).wait_send()
        mid_copy(j, middle).wait_send()
        near_copy(middle, j, core).wait_send()
        near_copy(other, j, core).wait_send()
    near_copy(other, quad, core).wait_send()
    mid_own.wait_send()
    near_own.wait_send()
    own.wait()


def subgrid_kernel(
    slots, count_ref, toff, summed, screen, pad, pad_t, ker, ker_t, observed,
    residual, coefficient, inner, model, adjoint, reduced, wide_t
):
    adjoint[...] = jnp.zeros_like(adjoint)
    residual[...] = jnp.zeros_like(residual)
    wide_t[...] = ker_t[...]
    sr, si = summed[0].astype(BF16), summed[1].astype(BF16)
    inner[0] = (dot(pad[0], sr) - dot(pad[1], si)).astype(BF16)
    inner[1] = (dot(pad[0], si) + dot(pad[1], sr)).astype(BF16)

    @pl.loop(0, 4)
    def _(c):
        rows = pl.ds(pl.multiple_of(c * 128, 128), 128)
        cos_value, sin_value = screen[0, rows, :], screen[1, rows, :]
        ir, ii = inner[0, rows, :], inner[1, rows, :]
        image_real = dot(ir, pad_t[0]) - dot(ii, pad_t[1])
        image_imag = dot(ir, pad_t[1]) + dot(ii, pad_t[0])
        model[0, rows, :] = (cos_value * image_real - sin_value * image_imag).astype(BF16)
        model[1, rows, :] = (cos_value * image_imag + sin_value * image_real).astype(BF16)

    count = count_ref[0]

    lanes = lax.broadcasted_iota(jnp.int32, (TV, TV), 1)
    blank = jnp.zeros((TV, TV), F32)

    def shifted(amount):
        low = pltpu.roll(ker[:, :TV], amount & 127, 1)
        high = pltpu.roll(ker[:, TV : 2 * TV], amount & 127, 1)
        inside = lanes >= amount
        return jnp.concatenate(
            [
                jnp.where(inside, low, blank).astype(BF16),
                jnp.where(inside, high, low).astype(BF16),
                jnp.where(inside, blank, high).astype(BF16),
            ],
            axis=1,
        )

    @pl.loop(0, (count + GROUP - 1) // GROUP)
    def _(step):
        slot = [step * GROUP + g for g in range(GROUP)]
        spans, ku, kv, kut = [], [], [], []
        for t in slot:
            ou, ov = toff[0, t], toff[1, t]
            u0 = pl.multiple_of(jnp.minimum(ou & ~127, 128), 128)
            v0 = pl.multiple_of(jnp.minimum(ov & ~127, 128), 128)
            spans.append((pl.ds(u0, SPAN), pl.ds(v0, SPAN)))
            ku.append(shifted(ou - u0))
            kv.append(shifted(ov - v0))
            kut.append(wide_t[pl.ds(128 - (ou - u0), SPAN), :].astype(BF16))
        left = [
            jnp.concatenate(
                [dot(ku[g], model[p, spans[g][0], spans[g][1]]).astype(BF16) for p in range(2)], axis=0
            )
            for g in range(GROUP)
        ]
        predicted = [dot_t(left[g], kv[g]) for g in range(GROUP)]
        rest = []
        for g, t in enumerate(slot):
            seen = observed[t].reshape(2 * TV, TV).astype(F32)
            value = (seen - predicted[g]).astype(BF16)
            rest.append(jnp.where(t < count, value, jnp.zeros_like(value)))
            residual[t] = rest[g].reshape(2, TV, TV)
        back = [dot(rest[g], kv[g]).astype(BF16) for g in range(GROUP)]
        spread = [[dot(kut[g], back[g][p * TV : p * TV + TV]) for p in range(2)] for g in range(GROUP)]
        for g in range(GROUP):
            for p in range(2):
                adjoint[p, spans[g][0], spans[g][1]] += spread[g][p]

    @pl.loop(0, 2)
    def _(c):
        cols = pl.ds(pl.multiple_of(c * 256, 256), 256)
        ar, ai = adjoint[0, :, cols], adjoint[1, :, cols]
        sc, ss = screen[0, :, cols], screen[1, :, cols]
        xr = (sc * ar + ss * ai).astype(BF16)
        xi = (sc * ai - ss * ar).astype(BF16)
        reduced[0, :, cols] = (dot(pad_t[0], xr) + dot(pad_t[1], xi)).astype(BF16)
        reduced[1, :, cols] = (dot(pad_t[0], xi) - dot(pad_t[1], xr)).astype(BF16)

    rr, ri = reduced[0], reduced[1]
    coefficient[0] = (dot(rr, pad[0]) + dot(ri, pad[1])).astype(BF16)
    coefficient[1] = (dot(ri, pad[0]) - dot(rr, pad[1])).astype(BF16)


def backward_kernel(n, foff, soff, piece, basis, taper, out, acc, spec, half, phase):
    phase[0], phase[1] = tapered_phase(foff, taper)
    lanes = lax.broadcasted_iota(jnp.int32, (M, M), 1)
    acc[...] = jnp.zeros_like(acc)

    @pl.loop(0, n)
    def _(s):
        sx, sy = soff[0, s], soff[1, s]
        tile, shift = sy >> 7, sy & 127
        rows = pl.ds(sx, M)
        kept = lanes >= shift
        pc, ps = phase[0], phase[1]
        real, imag = piece[s, 0].astype(F32), piece[s, 1].astype(F32)
        blank = jnp.zeros((M, M), F32)
        values = (pc * real + ps * imag, pc * imag - ps * real)
        for plane in range(2):
            turned = pltpu.roll(values[plane], shift, 1)
            acc[plane, tile, rows] += jnp.where(kept, turned, blank)
            acc[plane, tile + 1, rows] += jnp.where(kept, blank, turned)

    acc[:, 0] += acc[:, F // M]
    acc[:, 0 : F // M, 0:M] += acc[:, 0 : F // M, F:WIDE]
    for k in range(F // M):
        spec[:, :, k * M : k * M + M] = acc[:, k, 0:F].astype(BF16)

    @pl.loop(0, 2)
    def _(c):
        cols = pl.ds(pl.multiple_of(c * 256, 256), 256)
        xr, xi = spec[0, :, cols], spec[1, :, cols]
        half[0, :, cols] = (dot(basis[0], xr) + dot(basis[1], xi)).astype(BF16)
        half[1, :, cols] = (dot(basis[0], xi) - dot(basis[1], xr)).astype(BF16)

    @pl.loop(0, 2)
    def _(c):
        cols = pl.ds(pl.multiple_of(c * 256, 256), 256)
        br, bi = basis[0, :, cols], basis[1, :, cols]
        out[0, :, cols] = (dot(half[0], br) + dot(half[1], bi)).astype(BF16)
        out[1, :, cols] = (dot(half[1], br) - dot(half[0], bi)).astype(BF16)


SMEM_SPEC = pl.BlockSpec(memory_space=pltpu.SMEM)
VMEM_SPEC = pl.BlockSpec(memory_space=pltpu.VMEM)
HBM_SPEC = pl.BlockSpec(memory_space=pltpu.HBM)
DMA = pltpu.SemaphoreType.DMA


def per_device(facets, facet_offsets, subgrid_offsets, w_terms, tile_count, tile_offsets, observed):
    n = lax.axis_size("facet")
    quads = n // 4
    soff_t = subgrid_offsets.T
    slots = observed.shape[0]
    basis = jnp.asarray(basis_table())
    pad_np = padding_table(n)
    pad = jnp.asarray(pad_np)
    pad_t = jnp.asarray(np.ascontiguousarray(pad_np.transpose(0, 2, 1)))
    taper = jnp.asarray(taper_square())
    table = kernel_table()
    ker_t_np = np.zeros((4 * TV, TV), np.float32)
    ker_t_np[TV : 3 * TV] = table.T
    plain = pltpu.CompilerParams(vmem_limit_bytes=LIMIT)

    contrib = pl.pallas_call(
        functools.partial(forward_kernel, n),
        out_shape=jax.ShapeDtypeStruct((2, 2, quads, 2, M, M), BF16),
        in_specs=[HBM_SPEC] * 5,
        out_specs=VMEM_SPEC,
        scratch_shapes=[
            VMEM((2, F, F), BF16), VMEM((2, WIDE // M, WIDE, M), F32), VMEM((2, M, M), F32),
            pltpu.SMEM((1, 2), jnp.int32), pltpu.SMEM((2, n), jnp.int32),
            VMEM((2, F, F), BF16), VMEM((2, F, F), BF16), VMEM((M, M), F32), DMA((5,)),
        ],
        compiler_params=plain,
        name="forward",
    )(*[pltpu.with_memory_space_constraint(x, pltpu.HBM) for x in (facet_offsets, soff_t, facets[0], basis, taper)])

    summed, screen = pl.pallas_call(
        functools.partial(reduce_kernel, n),
        out_shape=(
            jax.ShapeDtypeStruct((2, M, M), F32), jax.ShapeDtypeStruct((2, SG, SG), F32),
        ),
        in_specs=[SMEM_SPEC, VMEM_SPEC],
        out_specs=(VMEM_SPEC, VMEM_SPEC),
        scratch_shapes=[VMEM((2, quads, 2, M, M), BF16)]
        + [VMEM((quads, 2, M, M), BF16)] * 4
        + [DMA((2, quads))] * 2
        + [DMA((quads,))] * 4,
        compiler_params=pltpu.CompilerParams(
            vmem_limit_bytes=LIMIT, collective_id=0, has_side_effects=True
        ),
        name="reduce",
    )(w_terms, contrib)

    residual, coefficient = pl.pallas_call(
        functools.partial(subgrid_kernel, slots),
        out_shape=(
            jax.ShapeDtypeStruct((slots, 2, TV, TV), BF16),
            jax.ShapeDtypeStruct((2, M, M), BF16),
        ),
        in_specs=[SMEM_SPEC] * 2 + [VMEM_SPEC] * 7,
        out_specs=(VMEM_SPEC, VMEM_SPEC),
        scratch_shapes=[
            VMEM((2, SG, M), BF16), VMEM((2, SG, SG), BF16),
            VMEM((2, SG, SG), F32), VMEM((2, M, SG), BF16), VMEM((4 * TV, TV), F32),
        ],
        compiler_params=plain,
        name="subgrid",
    )(
        tile_count, tile_offsets.T, summed, screen, pad, pad_t,
        jnp.asarray(table), jnp.asarray(ker_t_np), observed,
    )

    piece = pl.pallas_call(
        functools.partial(gather_kernel, n),
        out_shape=jax.ShapeDtypeStruct((n, 2, M, M), BF16),
        in_specs=[VMEM_SPEC],
        out_specs=VMEM_SPEC,
        scratch_shapes=[DMA((2, quads))] * 2 + [DMA((quads,))] * 4 + [DMA],
        compiler_params=pltpu.CompilerParams(
            vmem_limit_bytes=LIMIT, collective_id=1, has_side_effects=True
        ),
        name="gather",
    )(coefficient)

    update = pl.pallas_call(
        functools.partial(backward_kernel, n),
        out_shape=jax.ShapeDtypeStruct((2, F, F), BF16),
        in_specs=[SMEM_SPEC, SMEM_SPEC, VMEM_SPEC, VMEM_SPEC, VMEM_SPEC],
        out_specs=VMEM_SPEC,
        scratch_shapes=[
            VMEM((2, WIDE // M, WIDE, M), F32), VMEM((2, F, F), BF16), VMEM((2, F, F), BF16),
            VMEM((2, M, M), F32),
        ],
        compiler_params=plain,
        name="backward",
    )(facet_offsets, soff_t, piece, basis, taper)
    return (residual, update[None])


def solution(mesh):
    placed = (
        P(("groups", "facet"), None, None, None),
        P(("groups", "facet"), None),
        P("groups", None),
        P(("groups", "facet")),
        P(("groups", "facet")),
        P(("groups", "facet"), None),
        P(("groups", "facet"), None, None, None),
    )
    return jax.shard_map(
        per_device,
        mesh=mesh,
        in_specs=placed,
        out_specs=(
            P(("groups", "facet"), None, None, None),
            P(("groups", "facet"), None, None, None),
        ),
        check_vma=False,
    )
```

```python
import functools
import math

import jax
import jax.numpy as jnp
import ml_dtypes
import numpy as np
from jax import lax
from jax.experimental import pallas as pl
from jax.experimental.pallas import tpu as pltpu
from jax.sharding import PartitionSpec as P

F = 512
M = 128
SG = 512
TV = 128
SPAN = 384
WIDE = F + M
GROUP = 4

BF16 = jnp.bfloat16
F32 = jnp.float32
TWO_PI = 2.0 * math.pi
MESH = pl.DeviceIdType.MESH
VMEM = pltpu.VMEM
LIMIT = 48 * 1024 * 1024


def basis_table():
    index = np.arange(F)
    angle = -TWO_PI * (index[:, None] * index[None, :] % F) / F
    scale = 1.0 / math.sqrt(F)
    return np.stack([np.cos(angle) * scale, np.sin(angle) * scale]).astype(ml_dtypes.bfloat16)


def padding_table(facet_count):
    angle = TWO_PI * (np.arange(SG)[:, None] * np.arange(M)[None, :] % SG) / SG
    scale = (M * math.sqrt(facet_count)) ** (-0.5)
    return np.stack([np.cos(angle) * scale, np.sin(angle) * scale]).astype(ml_dtypes.bfloat16)


def taper_square():
    taper = 0.6 + 0.4 * np.sin(math.pi * (np.arange(M) + 0.5) / M)
    return (taper[:, None] * taper[None, :]).astype(np.float32)


def kernel_table():
    distance = np.arange(2 * TV)[None, :] - 2.0 * np.arange(TV)[:, None] - 1.0
    value = 0.75 * np.exp(-(distance / 1.5) * (distance / 1.5))
    return np.where(np.abs(distance) <= 4.0, value, 0.0).astype(ml_dtypes.bfloat16).astype(np.float32)


def dot(left, right):
    return jnp.dot(left, right, preferred_element_type=F32)


def dot_t(left, right):
    return lax.dot_general(left, right, (((1,), (1,)), ((), ())), preferred_element_type=F32)


def cos_sin_turns(turns):
    quarter = jnp.floor(turns * 4.0 + 0.5)
    y = (turns - quarter * 0.25) * TWO_PI
    y2 = y * y
    sine = y * (1.0 + y2 * (-1.0 / 6 + y2 * (1.0 / 120 + y2 * (-1.0 / 5040 + y2 * (1.0 / 362880)))))
    cosine = 1.0 + y2 * (
        -0.5 + y2 * (1.0 / 24 + y2 * (-1.0 / 720 + y2 * (1.0 / 40320 - y2 * (1.0 / 3628800))))
    )
    which = quarter.astype(jnp.int32) & 3
    odd = (which & 1) == 1
    first = jnp.where(odd, sine, cosine)
    second = jnp.where(odd, cosine, sine)
    cos_value = jnp.where((which == 1) | (which == 2), -first, first)
    sin_value = jnp.where(which >= 2, -second, second)
    return cos_value, sin_value


def tapered_phase(offset_ref, taper_ref):
    rows = lax.broadcasted_iota(jnp.int32, (M, M), 0)
    columns = lax.broadcasted_iota(jnp.int32, (M, M), 1)
    total = (rows * offset_ref[0, 0] + columns * offset_ref[0, 1]) & (F - 1)
    cos_value, sin_value = cos_sin_turns(total.astype(F32) * (1.0 / F))
    taper = taper_ref[...]
    return cos_value * taper, sin_value * taper


def forward_kernel(
    n, foff_h, soff_h, facet_h, basis_h, taper_h, out,
    half, spec, phase, foff, soff, facet, basis, taper, sems
):
    pairs = ((facet_h, facet), (basis_h, basis), (taper_h, taper), (foff_h, foff), (soff_h, soff))
    copies = [pltpu.make_async_copy(src, dst, sems.at[i]) for i, (src, dst) in enumerate(pairs)]
    for copy in copies:
        copy.start()
    for copy in copies:
        copy.wait()
    phase[0], phase[1] = tapered_phase(foff, taper)
    lanes = lax.broadcasted_iota(jnp.int32, (M, M), 1)

    @pl.loop(0, 2)
    def _(c):
        cols = pl.ds(pl.multiple_of(c * 256, 256), 256)
        br, bi = basis[0, :, cols], basis[1, :, cols]
        half[0, :, cols] = (dot(facet[0], br) - dot(facet[1], bi)).astype(BF16)
        half[1, :, cols] = (dot(facet[0], bi) + dot(facet[1], br)).astype(BF16)

    @pl.loop(0, 2)
    def _(c):
        cols = pl.ds(pl.multiple_of(c * 256, 256), 256)
        hr, hi = half[0, :, cols], half[1, :, cols]
        real = dot(basis[0], hr) - dot(basis[1], hi)
        imag = dot(basis[0], hi) + dot(basis[1], hr)
        for side in range(2):
            part = slice(side * M, side * M + M)
            spec[0, c * 2 + side, 0:F] = real[:, part]
            spec[1, c * 2 + side, 0:F] = imag[:, part]

    spec[:, 0 : F // M, F:WIDE] = spec[:, 0 : F // M, 0:M]
    spec[:, F // M] = spec[:, 0]

    @pl.loop(0, n, unroll=4)
    def _(s):
        sx, sy = soff[0, s], soff[1, s]
        tile, offset = sy >> 7, sy & 127
        shift = (M - offset) & 127
        kept = lanes < M - offset
        rows = pl.ds(sx, M)

        def window(plane):
            low = pltpu.roll(spec[plane, tile, rows], shift, 1)
            high = pltpu.roll(spec[plane, tile + 1, rows], shift, 1)
            return jnp.where(kept, low, high)

        real, imag = window(0), window(1)
        pc, ps = phase[0], phase[1]
        out[s & 1, (s >> 1) & 1, s >> 2, 0] = (pc * real - ps * imag).astype(BF16)
        out[s & 1, (s >> 1) & 1, s >> 2, 1] = (pc * imag + ps * real).astype(BF16)


def place(n):
    me = lax.axis_index("facet")
    quads = n // 4
    far_first = [1 + (t + quads // 2 - 1) % (quads - 1) for t in range(quads - 1)]
    return quads, me // 4, lax.rem(me // 2, 2), lax.rem(me, 2), far_first


def index(quad, middle, core):
    return quad * 4 + middle * 2 + core


def greet(peers):
    barrier = pltpu.get_barrier_semaphore()
    for peer in peers:
        pl.semaphore_signal(barrier, inc=1, device_id={"facet": peer}, device_id_type=MESH)
    pl.semaphore_wait(barrier, len(peers))


def send(src, dst, send_sem, recv_sem, peer):
    return pltpu.make_async_remote_copy(
        src_ref=src, dst_ref=dst, send_sem=send_sem, recv_sem=recv_sem,
        device_id={"facet": peer}, device_id_type=MESH,
    )


def fill_screen(w_value, screen):
    @pl.loop(0, 4)
    def _(c):
        rows = pl.ds(pl.multiple_of(c * 128, 128), 128)
        u = (lax.broadcasted_iota(jnp.int32, (128, SG), 0) + (c * 128 - 256)).astype(F32)
        v = (lax.broadcasted_iota(jnp.int32, (128, SG), 1) - 256).astype(F32)
        radius = (u * u + v * v) * (1.0 / (SG * SG))
        cos_value, sin_value = cos_sin_turns(w_value * (jnp.sqrt(1.0 + radius) - 1.0))
        screen[0, rows, :] = cos_value
        screen[1, rows, :] = sin_value


def reduce_kernel(
    n, w_ref, contrib, summed, screen, near, pair, mid, quad_sum, far,
    near_s, near_r, mid_s, mid_r, far_s, far_r
):
    quads, quad, middle, core, far_first = place(n)
    other = 1 - middle
    sibling, beside = index(quad, middle, 1 - core), index(quad, other, core)
    away = [lax.rem(quad + k, quads) for k in far_first]
    order = away + [quad]
    greet([index(j, middle, core) for j in away] + [beside, sibling])

    def near_copy(half, j):
        return send(contrib.at[1 - core, half, j], near.at[half, j], near_s.at[half, j], near_r.at[half, j], sibling)

    def mid_copy(j):
        return send(pair.at[j], mid.at[j], mid_s.at[j], mid_r.at[j], beside)

    def far_copy(j, slot):
        return send(quad_sum.at[j], far.at[slot], far_s.at[j], far_r.at[slot], index(j, middle, core))

    def near_sum(half, j):
        return contrib[core, half, j].astype(F32) + near[half, j].astype(F32)

    for half in (other, middle):
        for j in order:
            near_copy(half, j).start()
    for j in order:
        near_copy(other, j).wait_recv()
        pair[j] = near_sum(other, j).astype(BF16)
        mid_copy(j).start()
    for j in away:
        near_copy(middle, j).wait_recv()
        mid_copy(j).wait_recv()
        quad_sum[j] = (near_sum(middle, j) + mid[j].astype(F32)).astype(BF16)
        far_copy(j, quad).start()
    fill_screen(w_ref[0], screen)
    near_copy(middle, quad).wait_recv()
    mid_copy(quad).wait_recv()
    total = near_sum(middle, quad) + mid[quad].astype(F32)
    for j in reversed(away):
        far_copy(j, j).wait_recv()
        total = total + far[j].astype(F32)
    summed[...] = total
    for j in order:
        near_copy(other, j).wait_send()
        near_copy(middle, j).wait_send()
        mid_copy(j).wait_send()
    for j in away:
        far_copy(j, quad).wait_send()


def gather_kernel(n, mine, out, near_s, near_r, mid_s, mid_r, far_s, far_r, local):
    quads, quad, middle, core, far_first = place(n)
    other = 1 - middle
    me = index(quad, middle, core)
    sibling, beside = index(quad, middle, 1 - core), index(quad, other, core)
    away = [lax.rem(quad + k, quads) for k in far_first]
    back = [lax.rem(quad + quads - k, quads) for k in far_first]
    greet([index(j, middle, core) for j in away] + [beside, sibling])

    def far_copy(j, slot):
        return send(
            mine, out.at[index(slot, middle, core)], far_s.at[j], far_r.at[slot], index(j, middle, core)
        )

    def mid_copy(j, half):
        piece = out.at[index(j, half, core)]
        return send(piece, piece, mid_s.at[j], mid_r.at[j], beside)

    def near_copy(half, j, side):
        piece = out.at[index(j, half, side)]
        return send(piece, piece, near_s.at[half, j], near_r.at[half, j], sibling)

    for j in away:
        far_copy(j, quad).start()
    mid_own = send(mine, out.at[me], mid_s.at[quad], mid_r.at[quad], beside)
    mid_own.start()
    near_own = send(mine, out.at[me], near_s.at[middle, quad], near_r.at[middle, quad], sibling)
    near_own.start()
    own = pltpu.make_async_copy(mine, out.at[me], local)
    own.start()
    for j in back:
        far_copy(j, j).wait_recv()
        mid_copy(j, middle).start()
        near_copy(middle, j, core).start()
    for j in [quad] + back:
        mid_copy(j, other).wait_recv()
        near_copy(other, j, core).start()
    for half in (middle, other):
        for j in [quad] + back:
            near_copy(half, j, 1 - core).wait_recv()
    for j in away:
        far_copy(j, quad).wait_send()
        mid_copy(j, middle).wait_send()
        near_copy(middle, j, core).wait_send()
        near_copy(other, j, core).wait_send()
    near_copy(other, quad, core).wait_send()
    mid_own.wait_send()
    near_own.wait_send()
    own.wait()


def subgrid_kernel(
    slots, count_ref, toff, summed, screen, pad, pad_t, ker, ker_t, observed,
    residual, coefficient, inner, model, adjoint, reduced, wide_t
):
    adjoint[...] = jnp.zeros_like(adjoint)
    residual[...] = jnp.zeros_like(residual)
    wide_t[...] = ker_t[...]
    sr, si = summed[0].astype(BF16), summed[1].astype(BF16)
    inner[0] = (dot(pad[0], sr) - dot(pad[1], si)).astype(BF16)
    inner[1] = (dot(pad[0], si) + dot(pad[1], sr)).astype(BF16)

    @pl.loop(0, 4)
    def _(c):
        rows = pl.ds(pl.multiple_of(c * 128, 128), 128)
        cos_value, sin_value = screen[0, rows, :], screen[1, rows, :]
        ir, ii = inner[0, rows, :], inner[1, rows, :]
        image_real = dot(ir, pad_t[0]) - dot(ii, pad_t[1])
        image_imag = dot(ir, pad_t[1]) + dot(ii, pad_t[0])
        model[0, rows, :] = (cos_value * image_real - sin_value * image_imag).astype(BF16)
        model[1, rows, :] = (cos_value * image_imag + sin_value * image_real).astype(BF16)

    count = count_ref[0]

    lanes = lax.broadcasted_iota(jnp.int32, (TV, TV), 1)
    blank = jnp.zeros((TV, TV), F32)

    def shifted(amount):
        low = pltpu.roll(ker[:, :TV], amount & 127, 1)
        high = pltpu.roll(ker[:, TV : 2 * TV], amount & 127, 1)
        inside = lanes >= amount
        return jnp.concatenate(
            [
                jnp.where(inside, low, blank).astype(BF16),
                jnp.where(inside, high, low).astype(BF16),
                jnp.where(inside, blank, high).astype(BF16),
            ],
            axis=1,
        )

    @pl.loop(0, (count + GROUP - 1) // GROUP)
    def _(step):
        slot = [step * GROUP + g for g in range(GROUP)]
        spans, ku, kv, kut = [], [], [], []
        for t in slot:
            ou, ov = toff[0, t], toff[1, t]
            u0 = pl.multiple_of(jnp.minimum(ou & ~127, 128), 128)
            v0 = pl.multiple_of(jnp.minimum(ov & ~127, 128), 128)
            spans.append((pl.ds(u0, SPAN), pl.ds(v0, SPAN)))
            ku.append(shifted(ou - u0))
            kv.append(shifted(ov - v0))
            kut.append(wide_t[pl.ds(128 - (ou - u0), SPAN), :].astype(BF16))
        left = [
            jnp.concatenate(
                [dot(ku[g], model[p, spans[g][0], spans[g][1]]).astype(BF16) for p in range(2)], axis=0
            )
            for g in range(GROUP)
        ]
        predicted = [dot_t(left[g], kv[g]) for g in range(GROUP)]
        rest = []
        for g, t in enumerate(slot):
            seen = observed[t].reshape(2 * TV, TV).astype(F32)
            value = (seen - predicted[g]).astype(BF16)
            rest.append(jnp.where(t < count, value, jnp.zeros_like(value)))
            residual[t] = rest[g].reshape(2, TV, TV)
        back = [dot(rest[g], kv[g]).astype(BF16) for g in range(GROUP)]
        spread = [[dot(kut[g], back[g][p * TV : p * TV + TV]) for p in range(2)] for g in range(GROUP)]
        for g in range(GROUP):
            for p in range(2):
                adjoint[p, spans[g][0], spans[g][1]] += spread[g][p]

    @pl.loop(0, 2)
    def _(c):
        cols = pl.ds(pl.multiple_of(c * 256, 256), 256)
        ar, ai = adjoint[0, :, cols], adjoint[1, :, cols]
        sc, ss = screen[0, :, cols], screen[1, :, cols]
        xr = (sc * ar + ss * ai).astype(BF16)
        xi = (sc * ai - ss * ar).astype(BF16)
        reduced[0, :, cols] = (dot(pad_t[0], xr) + dot(pad_t[1], xi)).astype(BF16)
        reduced[1, :, cols] = (dot(pad_t[0], xi) - dot(pad_t[1], xr)).astype(BF16)

    rr, ri = reduced[0], reduced[1]
    coefficient[0] = (dot(rr, pad[0]) + dot(ri, pad[1])).astype(BF16)
    coefficient[1] = (dot(ri, pad[0]) - dot(rr, pad[1])).astype(BF16)


def backward_kernel(n, foff, soff, piece, basis, taper, out, acc, spec, half, phase):
    phase[0], phase[1] = tapered_phase(foff, taper)
    lanes = lax.broadcasted_iota(jnp.int32, (M, M), 1)
    acc[...] = jnp.zeros_like(acc)

    @pl.loop(0, n, unroll=4)
    def _(s):
        sx, sy = soff[0, s], soff[1, s]
        tile, shift = sy >> 7, sy & 127
        rows = pl.ds(sx, M)
        kept = lanes >= shift
        pc, ps = phase[0], phase[1]
        real, imag = piece[s, 0].astype(F32), piece[s, 1].astype(F32)
        blank = jnp.zeros((M, M), F32)
        values = (pc * real + ps * imag, pc * imag - ps * real)
        for plane in range(2):
            turned = pltpu.roll(values[plane], shift, 1)
            acc[plane, tile, rows] += jnp.where(kept, turned, blank)
            acc[plane, tile + 1, rows] += jnp.where(kept, blank, turned)

    acc[:, 0] += acc[:, F // M]
    acc[:, 0 : F // M, 0:M] += acc[:, 0 : F // M, F:WIDE]
    for k in range(F // M):
        spec[:, :, k * M : k * M + M] = acc[:, k, 0:F].astype(BF16)

    @pl.loop(0, 2)
    def _(c):
        cols = pl.ds(pl.multiple_of(c * 256, 256), 256)
        xr, xi = spec[0, :, cols], spec[1, :, cols]
        half[0, :, cols] = (dot(basis[0], xr) + dot(basis[1], xi)).astype(BF16)
        half[1, :, cols] = (dot(basis[0], xi) - dot(basis[1], xr)).astype(BF16)

    @pl.loop(0, 2)
    def _(c):
        cols = pl.ds(pl.multiple_of(c * 256, 256), 256)
        br, bi = basis[0, :, cols], basis[1, :, cols]
        out[0, :, cols] = (dot(half[0], br) + dot(half[1], bi)).astype(BF16)
        out[1, :, cols] = (dot(half[1], br) - dot(half[0], bi)).astype(BF16)


SMEM_SPEC = pl.BlockSpec(memory_space=pltpu.SMEM)
VMEM_SPEC = pl.BlockSpec(memory_space=pltpu.VMEM)
HBM_SPEC = pl.BlockSpec(memory_space=pltpu.HBM)
DMA = pltpu.SemaphoreType.DMA


def per_device(facets, facet_offsets, subgrid_offsets, w_terms, tile_count, tile_offsets, observed):
    n = lax.axis_size("facet")
    quads = n // 4
    soff_t = subgrid_offsets.T
    slots = observed.shape[0]
    basis = jnp.asarray(basis_table())
    pad_np = padding_table(n)
    pad = jnp.asarray(pad_np)
    pad_t = jnp.asarray(np.ascontiguousarray(pad_np.transpose(0, 2, 1)))
    taper = jnp.asarray(taper_square())
    table = kernel_table()
    ker_t_np = np.zeros((4 * TV, TV), np.float32)
    ker_t_np[TV : 3 * TV] = table.T
    plain = pltpu.CompilerParams(vmem_limit_bytes=LIMIT)

    contrib = pl.pallas_call(
        functools.partial(forward_kernel, n),
        out_shape=jax.ShapeDtypeStruct((2, 2, quads, 2, M, M), BF16),
        in_specs=[HBM_SPEC] * 5,
        out_specs=VMEM_SPEC,
        scratch_shapes=[
            VMEM((2, F, F), BF16), VMEM((2, WIDE // M, WIDE, M), F32), VMEM((2, M, M), F32),
            pltpu.SMEM((1, 2), jnp.int32), pltpu.SMEM((2, n), jnp.int32),
            VMEM((2, F, F), BF16), VMEM((2, F, F), BF16), VMEM((M, M), F32), DMA((5,)),
        ],
        compiler_params=plain,
        name="forward",
    )(*[pltpu.with_memory_space_constraint(x, pltpu.HBM) for x in (facet_offsets, soff_t, facets[0], basis, taper)])

    summed, screen = pl.pallas_call(
        functools.partial(reduce_kernel, n),
        out_shape=(
            jax.ShapeDtypeStruct((2, M, M), F32), jax.ShapeDtypeStruct((2, SG, SG), F32),
        ),
        in_specs=[SMEM_SPEC, VMEM_SPEC],
        out_specs=(VMEM_SPEC, VMEM_SPEC),
        scratch_shapes=[VMEM((2, quads, 2, M, M), BF16)]
        + [VMEM((quads, 2, M, M), BF16)] * 4
        + [DMA((2, quads))] * 2
        + [DMA((quads,))] * 4,
        compiler_params=pltpu.CompilerParams(
            vmem_limit_bytes=LIMIT, collective_id=0, has_side_effects=True
        ),
        name="reduce",
    )(w_terms, contrib)

    residual, coefficient = pl.pallas_call(
        functools.partial(subgrid_kernel, slots),
        out_shape=(
            jax.ShapeDtypeStruct((slots, 2, TV, TV), BF16),
            jax.ShapeDtypeStruct((2, M, M), BF16),
        ),
        in_specs=[SMEM_SPEC] * 2 + [VMEM_SPEC] * 7,
        out_specs=(VMEM_SPEC, VMEM_SPEC),
        scratch_shapes=[
            VMEM((2, SG, M), BF16), VMEM((2, SG, SG), BF16),
            VMEM((2, SG, SG), F32), VMEM((2, M, SG), BF16), VMEM((4 * TV, TV), F32),
        ],
        compiler_params=plain,
        name="subgrid",
    )(
        tile_count, tile_offsets.T, summed, screen, pad, pad_t,
        jnp.asarray(table), jnp.asarray(ker_t_np), observed,
    )

    piece = pl.pallas_call(
        functools.partial(gather_kernel, n),
        out_shape=jax.ShapeDtypeStruct((n, 2, M, M), BF16),
        in_specs=[VMEM_SPEC],
        out_specs=VMEM_SPEC,
        scratch_shapes=[DMA((2, quads))] * 2 + [DMA((quads,))] * 4 + [DMA],
        compiler_params=pltpu.CompilerParams(
            vmem_limit_bytes=LIMIT, collective_id=1, has_side_effects=True
        ),
        name="gather",
    )(coefficient)

    update = pl.pallas_call(
        functools.partial(backward_kernel, n),
        out_shape=jax.ShapeDtypeStruct((2, F, F), BF16),
        in_specs=[SMEM_SPEC, SMEM_SPEC, VMEM_SPEC, VMEM_SPEC, VMEM_SPEC],
        out_specs=VMEM_SPEC,
        scratch_shapes=[
            VMEM((2, WIDE // M, WIDE, M), F32), VMEM((2, F, F), BF16), VMEM((2, F, F), BF16),
            VMEM((2, M, M), F32),
        ],
        compiler_params=plain,
        name="backward",
    )(facet_offsets, soff_t, piece, basis, taper)
    return (residual, update[None])


def solution(mesh):
    placed = (
        P(("groups", "facet"), None, None, None),
        P(("groups", "facet"), None),
        P("groups", None),
        P(("groups", "facet")),
        P(("groups", "facet")),
        P(("groups", "facet"), None),
        P(("groups", "facet"), None, None, None),
    )
    return jax.shard_map(
        per_device,
        mesh=mesh,
        in_specs=placed,
        out_specs=(
            P(("groups", "facet"), None, None, None),
            P(("groups", "facet"), None, None, None),
        ),
        check_vma=False,
    )
```
